128 devices in a mesh: row: 8 (over z, core), col: 16 (over y, x).
Axes of the slice: x: 4, y: 4, z: 4, core: 2. Of those that a mesh axis runs over, the one named last changes fastest.
Arguments:
- stored_blocks: float32 [8, 16, 2, 14, 256, 256], P('row', 'col'), may hold values from -0.0390625 to 0.0390625
- onsite: float32 [8, 16, 2, 256], P('row', 'col'), may hold values from 0.05 to 0.95
- bond_mask: int32 [8, 16, 2, 13], P('row', 'col'), may hold values 0 or 1
Outputs:
- purified: float32 [8, 16, 2, 14, 256, 256], P('row', 'col')
The draws below stay inside these ranges and needn't reach their ends.
All inputs are finite; a program needn't handle non-finite values. No bound on the sum of `bond_mask` on one device may be relied on, other than what follows from the above.
Results may differ from the reference program's by a relative error of at most 0.00024.
Values sent between devices are 32-bit elements; how exact they have to be, the bound alone decides.
A program may use at most 448 MiB of HBM per device.

```python
import jax
import jax.numpy as jnp
from jax import lax

B = 256
SLOTS = 14
NOFF = 13
NX = 8
NY = 16
NZ = 2
NOCC = 32768


def touch_ends(result, key, low, top_value):
    longest = result.shape.index(max(result.shape))
    spots = []
    for shift in (0, 1):
        where = [jax.random.randint(jax.random.fold_in(key, axis), (), 0, length) for axis, length in enumerate(result.shape)]
        where[longest] = (where[longest] + shift) % result.shape[longest]
        spots.append(tuple(where))
    return result.at[spots[0]].set(low).at[spots[1]].set(top_value)


def levels(rng, extent, pieces, least, high):
    loudness, own = 1.0, jax.random.fold_in(rng, 6)
    for axis_at, shards_of in pieces:
        steps = jnp.exp(jax.random.uniform(jax.random.fold_in(own, axis_at), (shards_of,), jnp.float32, least / len(pieces), high / len(pieces)))
        loudness = loudness * jnp.repeat(steps, extent[axis_at] // shards_of).reshape([-1 if axis == axis_at else 1 for axis in range(len(extent))])
    return loudness


def normal_values(rng, extent, spread, most, shards=(), held_as=jnp.bfloat16):
    values = spread * jax.random.normal(rng, extent, jnp.float32)
    if shards:
        values = values * levels(rng, extent, shards, -0.22, 0.18)
    return jnp.clip(values, -most, most).astype(held_as)


def setup_inputs(seed: int = 0) -> dict:
    seeds = jax.random.split(jax.random.key(seed), 4)
    stored_blocks = normal_values(seeds[0], (NX, NY, NZ, SLOTS, B, B), ((88 * B) ** -0.5), 0.0390625, ((0, 8), (1, 16)), jnp.float32)
    onsite = jnp.clip(0.05 + 0.9 * jax.random.uniform(seeds[1], (NX, NY, NZ, B), jnp.float32) ** levels(seeds[1], (NX, NY, NZ, B), ((0, 8), (1, 16)), -0.2, 0.2), 0.05, 0.95)
    bond_mask = touch_ends((jax.random.randint(seeds[2], (NX, NY, NZ, NOFF), 0, 13) < 7).astype(jnp.int32), jax.random.fold_in(seeds[2], 1), 0, 1)
    return dict(stored_blocks=stored_blocks, onsite=onsite, bond_mask=bond_mask)


def offset_list():
    return [(step_x, step_y, step_z) for step_x in (-1, 0, 1) for step_y in (-1, 0, 1) for step_z in (-1, 0, 1) if (step_x, step_y, step_z) > (0, 0, 0)]


def slot_number(offset):
    return offset_list().index(offset) + 1


def shift_cells(array, step_x, step_y, step_z):
    moved = jnp.roll(array, (-step_x, -step_y), axis=(0, 1))
    if step_z == 1:
        moved = jnp.concatenate([moved[:, :, 1:], jnp.zeros_like(moved[:, :, :1])], axis=2)
    elif step_z == -1:
        moved = jnp.concatenate([jnp.zeros_like(moved[:, :, :1]), moved[:, :, :-1]], axis=2)
    return moved


def stored_at(blocks_list, offset):
    if offset == (0, 0, 0):
        return blocks_list[0]
    if offset > (0, 0, 0):
        return blocks_list[slot_number(offset)]
    mirror = (-offset[0], -offset[1], -offset[2])
    return jnp.swapaxes(shift_cells(blocks_list[slot_number(mirror)], offset[0], offset[1], offset[2]), 3, 4)


def reference(stored_blocks, onsite, bond_mask):
    offsets = offset_list()
    zplace = jnp.arange(NZ)
    leading = stored_blocks[:, :, :, 0]
    diagonal = 0.5 * (leading + jnp.swapaxes(leading, 3, 4)) + jnp.eye(B, dtype=jnp.float32) * onsite[..., None, :]
    blocks_list = [diagonal]
    keep_list = [jnp.ones(onsite.shape[:3], jnp.float32)]
    for position, offset in enumerate(offsets):
        inside = ((zplace + offset[2] >= 0) & (zplace + offset[2] < NZ)).astype(jnp.float32)
        keep_now = bond_mask[..., position].astype(jnp.float32) * inside[None, None, :]
        keep_list.append(keep_now)
        blocks_list.append(stored_blocks[:, :, :, position + 1] * keep_now[..., None, None])
    trace_one = jnp.sum(jnp.trace(diagonal, axis1=3, axis2=4))
    trace_two = jnp.sum(diagonal * diagonal)
    for blocks_now in blocks_list[1:]:
        trace_two = trace_two + 2.0 * jnp.sum(blocks_now * blocks_now)
    all_offsets = [(step_x, step_y, step_z) for step_x in (-1, 0, 1) for step_y in (-1, 0, 1) for step_z in (-1, 0, 1)]
    squares = []
    for target_offset in [(0, 0, 0)] + offsets:
        running = jnp.zeros_like(diagonal)
        for middle in all_offsets:
            remainder = (target_offset[0] - middle[0], target_offset[1] - middle[1], target_offset[2] - middle[2])
            if max(abs(remainder[0]), abs(remainder[1]), abs(remainder[2])) > 1:
                continue
            left_term = stored_at(blocks_list, middle)
            right_term = shift_cells(stored_at(blocks_list, remainder), middle[0], middle[1], middle[2])
            running = running + jnp.einsum("xyzab,xyzbc->xyzac", left_term, right_term, precision=lax.Precision.HIGHEST)
        squares.append(running)
    steering = jax.nn.sigmoid((jnp.abs(trace_two - NOCC) - jnp.abs(2.0 * trace_one - trace_two - NOCC)) / B)
    outputs = []
    for slot_id in range(len(blocks_list)):
        mixed = squares[slot_id] + 2.0 * steering * (blocks_list[slot_id] - squares[slot_id])
        outputs.append(keep_list[slot_id][..., None, None] * mixed)
    return jnp.stack(outputs, axis=3)
```

```python
import jax
import jax.numpy as jnp
from jax import lax
from jax.experimental import pallas as pl
from jax.experimental.pallas import tpu as pltpu
from jax.sharding import PartitionSpec as P

MESH = pl.DeviceIdType.MESH
F32 = jnp.float32
BF16 = jnp.bfloat16
B = 256
W2 = 2 * B

DG, ER, ML, ZD, PR = range(5)
MIDDLE = {ER: 3, ML: 6, ZD: 9, PR: 12}
QQ = 5

(P_L, E_L, Q_L, M_R, Z_R, D_R, Z_U, P_U, P_UL, M_UR, Z_UR, E_W, D_W, E_WL, D_WR) = range(15)
NRX = 15
ET = 5


def sp(rx):
    return 6 + rx


QUADS = ((0, 0), (0, 1), (1, 0), (1, 1))
DQUADS = (0, 1, 3)


def block_slot(t, z, z2):
    return MIDDLE[t] + z2 - z


def kernel(stored, onsite, mask, out, own, rx, hi, lo, y, zero, part, gath, steer,
           in_sem, out_sem, send_sem, recv_sem, ar_send, ar_recv):
    row = lax.axis_index("row")
    col = lax.axis_index("col")
    nrow = lax.axis_size("row")
    ncol = lax.axis_size("col")
    right = (row, lax.rem(col + 1, ncol))
    left = (row, lax.rem(col + ncol - 1, ncol))
    down = (lax.rem(row + 1, nrow), col)
    up = (lax.rem(row + nrow - 1, nrow), col)
    xs = lax.rem(col, 4)
    ys = col // 4
    cs = lax.rem(row, 2)
    zs = row // 2
    x_peers = [(row, ys * 4 + lax.rem(xs + j, 4)) for j in (1, 2, 3)]
    y_peers = [(row, lax.rem(ys + j, 4) * 4 + xs) for j in (1, 2, 3)]
    z_peers = [(lax.rem(zs + j, 4) * 2 + cs, col) for j in (1, 2, 3)]
    core_peer = (zs * 2 + 1 - cs, col)

    loads = {}
    for t in (PR, ML, ER, ZD):
        for q, (z, z2) in enumerate(QUADS):
            loads[t, q] = pltpu.make_async_copy(
                stored.at[z, block_slot(t, z, z2)],
                own.at[t, pl.ds(z * B, B), pl.ds(z2 * B, B)],
                in_sem.at[(t - 1) * 4 + q],
            )
    for n, (q, z, slot) in enumerate(((0, 0, 0), (1, 0, 1), (3, 1, 0))):
        i, j = QUADS[q]
        loads[DG, q] = pltpu.make_async_copy(
            stored.at[z, slot], own.at[DG, pl.ds(i * B, B), pl.ds(j * B, B)], in_sem.at[16 + n]
        )
    for copy in loads.values():
        copy.start()

    barrier = pltpu.get_barrier_semaphore()
    greeted = [right, left, down, up] + x_peers + y_peers + z_peers + [core_peer]
    for peer in greeted:
        pl.semaphore_signal(barrier, inc=1, device_id=peer, device_id_type=MESH)

    zero[...] = jnp.zeros_like(zero)

    def put_split(k, rows, cols, value):
        high = value.astype(BF16)
        hi[k, rows, cols] = high
        lo[k, rows, cols] = (value - high.astype(F32)).astype(BF16)

    def strips(start, strip):
        return pl.ds(pl.multiple_of(start + strip, 8), 64)

    squares = jnp.zeros((8, B), F32)
    for t in (PR, ML, ER, ZD):
        for q, (z, z2) in enumerate(QUADS):
            loads[t, q].wait()
            keep = mask[z, block_slot(t, z, z2) - 1].astype(F32)
            cols = pl.ds(z2 * B, B)

            def strip_step(s, total, t=t, z=z, cols=cols, keep=keep):
                rows = pl.ds(pl.multiple_of(z * B + s * 64, 64), 64)
                value = own[t, rows, cols] * keep
                own[t, rows, cols] = value
                put_split(t, rows, cols, value)
                return total + jnp.sum((value * value).reshape(8, 8, B), axis=0)

            squares = lax.fori_loop(0, 4, strip_step, squares)
    squares = 2.0 * squares
    trace = jnp.zeros((8, B), F32)
    diag = lax.broadcasted_iota(jnp.int32, (B, B), 0) == lax.broadcasted_iota(jnp.int32, (B, B), 1)
    for z, q in ((0, 0), (1, 3)):
        loads[DG, q].wait()
        here = pl.ds(z * B, B)
        raw = own[DG, here, here]
        value = 0.5 * (raw + raw.T) + jnp.where(diag, onsite[z : z + 1, :], 0.0)
        own[DG, here, here] = value
        put_split(DG, here, here, value)
        squares = squares + jnp.sum((value * value).reshape(32, 8, B), axis=0)
        trace = trace + jnp.sum(jnp.where(diag, value, 0.0).reshape(32, 8, B), axis=0)
    loads[DG, 1].wait()
    top, low = pl.ds(0, B), pl.ds(B, B)
    value = own[DG, top, low] * mask[0, 0].astype(F32)
    own[DG, top, low] = value
    put_split(DG, top, low, value)
    squares = squares + 2.0 * jnp.sum((value * value).reshape(32, 8, B), axis=0)
    flipped = value.T
    own[DG, low, top] = flipped
    put_split(DG, low, top, flipped)
    part[0, 0:8, :] = trace
    part[0, 8:16, :] = squares

    pl.semaphore_wait(barrier, len(greeted))

    small = []

    def send_part(stage, peers, base):
        copies = []
        for n, peer in enumerate(peers):
            copy = pltpu.make_async_remote_copy(
                src_ref=part.at[stage],
                dst_ref=gath.at[base + n],
                send_sem=ar_send.at[base + n],
                recv_sem=ar_recv.at[base + n],
                device_id=peer,
                device_id_type=MESH,
            )
            copy.start()
            copies.append(copy)
        small.extend(copies)
        return copies

    def add_parts(stage, copies, base):
        total = part[stage]
        for n, copy in enumerate(copies):
            copy.wait_recv()
            total = total + gath[base + n]
        part[stage + 1] = total

    sent = {}

    def send(source, rxi, q, peer):
        i, j = QUADS[q]
        where = (pl.ds(i * B, B), pl.ds(j * B, B))
        copy = pltpu.make_async_remote_copy(
            src_ref=source(*where),
            dst_ref=rx.at[(rxi,) + where],
            send_sem=send_sem.at[rxi * 4 + q],
            recv_sem=recv_sem.at[rxi * 4 + q],
            device_id=peer,
            device_id_type=MESH,
        )
        copy.start()
        sent[rxi, q] = copy

    def from_own(t):
        return lambda rows, cols: own.at[t, rows, cols]

    def from_rx(k):
        return lambda rows, cols: rx.at[k, rows, cols]

    def from_y(k):
        return lambda rows, cols: y.at[k, rows, cols]

    def prep(rxi, q, flip=False, keep=True):
        i, j = QUADS[q]

        def strip_step(s, carry):
            offset = pl.multiple_of(s * 128, 128)
            value = rx[rxi, pl.ds(i * B + offset, 128), pl.ds(j * B, B)]
            if keep:
                put_split(sp(rxi), pl.ds(i * B + offset, 128), pl.ds(j * B, B), value)
            if flip:
                put_split(sp(rxi), pl.ds(j * B, B), pl.ds(i * B + offset, 128), value.T)
            return carry

        lax.fori_loop(0, 2, strip_step, 0)

    def take(rxi, quads=range(4), forward=None, **how):
        for q in quads:
            sent[rxi, q].wait_recv()
            if forward is not None:
                send(from_rx(rxi), forward[0], q, forward[1])
            prep(rxi, q, **how)

    def take_t(rxi, quads=range(4), forward=None):
        take(rxi, quads, forward, flip=True, keep=False)

    def take_d(rxi, quads=DQUADS, forward=None):
        for q in quads:
            take(rxi, (q,), forward, flip=q == 1)

    def products(yi, terms, first=False):
        def tile(step, carry):
            if yi == DG:
                m, n = step // 2, (step + 1) // 2
            else:
                m, n = step // 2, step % 2
            rows = pl.ds(pl.multiple_of(m * B, B), B)
            cols = pl.ds(pl.multiple_of(n * B, B), B)
            total = None if first else y[yi, rows, cols]
            for a, b, turned in terms:
                a_hi = hi[a, rows, :]
                a_lo = lo[a, rows, :]
                if turned:
                    b_hi, b_lo = hi[b, cols, :], lo[b, cols, :]
                    dims = (((1,), (1,)), ((), ()))
                else:
                    b_hi, b_lo = hi[b, :, cols], lo[b, :, cols]
                    dims = (((1,), (0,)), ((), ()))
                for u, v in ((a_hi, b_hi), (a_hi, b_lo), (a_lo, b_hi)):
                    term = lax.dot_general(u, v, dims, preferred_element_type=F32)
                    total = term if total is None else total + term
            y[yi, rows, cols] = total
            return carry

        lax.fori_loop(0, 3 if yi == DG else 4, tile, 0)

    outs = []

    def finish(yi, extra=None):
        quads = DQUADS if yi == DG else range(4)
        for q in quads:
            z, z2 = QUADS[q]
            if yi == DG:
                slot = 1 if q == 1 else 0
            else:
                slot = block_slot(yi, z, z2)
            if extra is not None:
                sent[extra, q].wait_recv()
            keep = mask[z, slot - 1].astype(F32) if slot else None

            def strip_step(s, carry, z=z, z2=z2, keep=keep):
                rows = pl.ds(pl.multiple_of(z * B + s * 64, 64), 64)
                cols = pl.ds(z2 * B, B)
                value = y[yi, rows, cols]
                if extra is not None:
                    value = value + rx[extra, rows, cols]
                value = value + steer[0:1, :] * (own[yi, rows, cols] - value)
                if keep is not None:
                    value = value * keep
                y[yi, rows, cols] = value
                return carry

            lax.fori_loop(0, 4, strip_step, 0)
            copy = pltpu.make_async_copy(
                y.at[yi, pl.ds(z * B, B), pl.ds(z2 * B, B)],
                out.at[z, slot],
                out_sem.at[z * 14 + slot],
            )
            copy.start()
            outs.append(copy)

    x_parts = send_part(0, x_peers, 0)
    for q in range(4):
        send(from_own(PR), P_L, q, right)
        send(from_own(ML), M_R, q, left)
    for q in range(4):
        send(from_own(ER), E_L, q, right)
        send(from_own(ZD), Z_R, q, left)
    for q in DQUADS:
        send(from_own(DG), D_R, q, left)

    for z, slots in ((0, (2, 5, 8, 11)), (1, (1, 4, 7, 10, 13))):
        for slot in slots:
            copy = pltpu.make_async_copy(zero, out.at[z, slot], out_sem.at[z * 14 + slot])
            copy.start()
            outs.append(copy)

    products(ER, [(DG, ER, False)], first=True)
    add_parts(0, x_parts, 0)
    z_parts = send_part(1, z_peers, 3)

    for q in range(4):
        send(from_own(ZD), Z_U, q, down)
        send(from_own(ER), E_W, q, up)
    for q in DQUADS:
        send(from_own(DG), D_W, q, up)
    for q in range(4):
        send(from_own(PR), P_U, q, down)

    for q, (i, j) in enumerate(QUADS):
        value = own[ER, pl.ds(i * B, B), pl.ds(j * B, B)].T
        put_split(ET, pl.ds(j * B, B), pl.ds(i * B, B), value)

    products(QQ, [(ET, ZD, False)], first=True)
    add_parts(1, z_parts, 3)
    y_parts = send_part(2, y_peers, 6)
    products(DG, [(DG, DG, False), (ER, ER, True), (ML, ML, True)], first=True)
    add_parts(2, y_parts, 6)
    core_part = send_part(3, [core_peer], 9)

    take(P_L, (0,), (P_UL, down))
    take(M_R, (0,), (M_UR, down))
    products(DG, [(ZD, ZD, True), (PR, PR, True)])
    core_part[0].wait_recv()
    total = part[3] + gath[9]
    t1 = jnp.sum(total[0:8, :])
    t2 = jnp.sum(total[8:16, :])
    goal = float(nrow * ncol * B)
    lean = (jnp.abs(t2 - goal) - jnp.abs(2.0 * t1 - t2 - goal)) / B
    steer[...] = 2.0 / (1.0 + jnp.exp(-jnp.full((8, B), lean, F32)))

    take(P_L, (1,), (P_UL, down))
    take(M_R, (1,), (M_UR, down))
    products(ML, [(DG, ML, False)], first=True)
    products(ZD, [(DG, ZD, False)], first=True)
    take(P_L, (2,), (P_UL, down))
    take(M_R, (2,), (M_UR, down))
    products(PR, [(DG, PR, False)], first=True)
    take_d(D_W)
    take(P_L, (3,), (P_UL, down))
    take(M_R, (3,), (M_UR, down))
    products(QQ, [(sp(M_R), sp(D_W), False)])
    for q in range(4):
        send(from_y(QQ), Q_L, q, right)

    take(E_W)
    take_t(Z_U)
    take(P_U)
    take_t(E_L, (0,), (E_WL, up))
    take(Z_R, (0,), (Z_UR, down))
    products(ZD, [(ZD, sp(D_W), False), (ER, sp(M_R), False), (PR, sp(E_W), True)])
    take_t(E_L, (1,), (E_WL, up))
    take(Z_R, (1,), (Z_UR, down))
    products(ER, [(ZD, sp(M_R), True), (sp(Z_U), sp(P_U), False)])
    products(PR, [(ZD, sp(E_W), False)])
    take_t(E_L, (2,), (E_WL, up))
    take(Z_R, (2,), (Z_UR, down))
    products(DG, [(sp(Z_U), sp(Z_U), True)])
    take_t(E_L, (3,), (E_WL, up))
    take(Z_R, (3,), (Z_UR, down))
    products(ZD, [(sp(E_L), sp(P_L), False)])
    products(ER, [(PR, sp(Z_R), True)])
    take_t(P_UL)
    take_t(M_UR)
    take_d(D_R, (0,), (D_WR, up))
    products(PR, [(ER, sp(Z_R), False)])
    take_d(D_R, (1,), (D_WR, up))
    products(DG, [(sp(E_L), sp(E_L), True), (sp(P_UL), sp(P_UL), True), (sp(M_UR), sp(M_UR), True)])
    take_d(D_R, (3,), (D_WR, up))
    finish(DG)
    take(Z_UR)
    products(ER, [(ER, sp(D_R), False), (sp(M_UR), sp(Z_UR), False)])
    finish(ER)
    take(E_WL)
    products(ZD, [(ML, sp(E_WL), False)])
    finish(ZD)
    products(ML, [(ZD, sp(E_WL), True)])
    take_d(D_WR)
    products(PR, [(PR, sp(D_WR), False)])
    finish(PR)
    finish(ML, Q_L)

    for copy in outs:
        copy.wait()
    for copy in small:
        copy.wait_send()
    for copy in sent.values():
        copy.wait_send()


def shards(stored_blocks, onsite, bond_mask):
    shape = stored_blocks.shape
    result = pl.pallas_call(
        kernel,
        out_shape=jax.ShapeDtypeStruct(shape[2:], F32),
        in_specs=[
            pl.BlockSpec(memory_space=pl.ANY),
            pl.BlockSpec(memory_space=pltpu.VMEM),
            pl.BlockSpec(memory_space=pltpu.SMEM),
        ],
        out_specs=pl.BlockSpec(memory_space=pl.ANY),
        scratch_shapes=[
            pltpu.VMEM((5, W2, W2), F32),
            pltpu.VMEM((NRX, W2, W2), F32),
            pltpu.VMEM((6 + NRX, W2, W2), BF16),
            pltpu.VMEM((6 + NRX, W2, W2), BF16),
            pltpu.VMEM((6, W2, W2), F32),
            pltpu.VMEM((B, B), F32),
            pltpu.VMEM((4, 16, B), F32),
            pltpu.VMEM((10, 16, B), F32),
            pltpu.VMEM((8, B), F32),
            pltpu.SemaphoreType.DMA((19,)),
            pltpu.SemaphoreType.DMA((28,)),
            pltpu.SemaphoreType.DMA((NRX * 4,)),
            pltpu.SemaphoreType.DMA((NRX * 4,)),
            pltpu.SemaphoreType.DMA((10,)),
            pltpu.SemaphoreType.DMA((10,)),
        ],
        compiler_params=pltpu.CompilerParams(
            collective_id=0, has_side_effects=True, vmem_limit_bytes=62 * 1024 * 1024
        ),
        name="sp2_step",
    )(stored_blocks[0, 0], onsite[0, 0], bond_mask[0, 0])
    return result[None, None]


def solution(mesh):
    in_specs = (
        P("row", "col", None, None, None, None),
        P("row", "col", None, None),
        P("row", "col", None, None),
    )
    out_specs = P("row", "col", None, None, None, None)
    return jax.shard_map(shards, mesh=mesh, in_specs=in_specs, out_specs=out_specs, check_vma=False)
```

```python
import jax
import jax.numpy as jnp
from jax import lax
from jax.experimental import pallas as pl
from jax.experimental.pallas import tpu as pltpu
from jax.sharding import PartitionSpec as P

MESH = pl.DeviceIdType.MESH
F32 = jnp.float32
BF16 = jnp.bfloat16
B = 256
W2 = 2 * B

DG, ER, ML, ZD, PR = range(5)
MIDDLE = {ER: 3, ML: 6, ZD: 9, PR: 12}
QQ = 5

(P_L, E_L, Q_L, M_R, Z_R, D_R, Z_U, P_U, P_UL, M_UR, Z_UR, E_W, D_W, E_WL, D_WR) = range(15)
NRX = 15
ET = 5


def sp(rx):
    return 6 + rx


QUADS = ((0, 0), (0, 1), (1, 0), (1, 1))
DQUADS = (0, 1, 3)


def block_slot(t, z, z2):
    return MIDDLE[t] + z2 - z


def kernel(stored, onsite, mask, out, own, rx, hi, lo, y, zero, part, gath, steer,
           in_sem, out_sem, send_sem, recv_sem, ar_send, ar_recv):
    row = lax.axis_index("row")
    col = lax.axis_index("col")
    nrow = lax.axis_size("row")
    ncol = lax.axis_size("col")
    right = (row, lax.rem(col + 1, ncol))
    left = (row, lax.rem(col + ncol - 1, ncol))
    down = (lax.rem(row + 1, nrow), col)
    up = (lax.rem(row + nrow - 1, nrow), col)
    col_peers = [(row, lax.rem(col + j, ncol)) for j in range(1, ncol)]
    row_peers = [(lax.rem(row + j, nrow), col) for j in range(1, nrow)]

    loads = {}
    for t in (PR, ML, ER, ZD):
        for q, (z, z2) in enumerate(QUADS):
            loads[t, q] = pltpu.make_async_copy(
                stored.at[z, block_slot(t, z, z2)],
                own.at[t, pl.ds(z * B, B), pl.ds(z2 * B, B)],
                in_sem.at[(t - 1) * 4 + q],
            )
    for n, (q, z, slot) in enumerate(((0, 0, 0), (1, 0, 1), (3, 1, 0))):
        i, j = QUADS[q]
        loads[DG, q] = pltpu.make_async_copy(
            stored.at[z, slot], own.at[DG, pl.ds(i * B, B), pl.ds(j * B, B)], in_sem.at[16 + n]
        )
    for copy in loads.values():
        copy.start()

    barrier = pltpu.get_barrier_semaphore()
    greeted = col_peers + row_peers
    for peer in greeted:
        pl.semaphore_signal(barrier, inc=1, device_id=peer, device_id_type=MESH)

    zero[...] = jnp.zeros_like(zero)

    def put_split(k, rows, cols, value):
        high = value.astype(BF16)
        hi[k, rows, cols] = high
        lo[k, rows, cols] = (value - high.astype(F32)).astype(BF16)

    sent = {}

    def send(source, rxi, q, peer):
        i, j = QUADS[q]
        where = (pl.ds(i * B, B), pl.ds(j * B, B))
        copy = pltpu.make_async_remote_copy(
            src_ref=source(*where),
            dst_ref=rx.at[(rxi,) + where],
            send_sem=send_sem.at[rxi * 4 + q],
            recv_sem=recv_sem.at[rxi * 4 + q],
            device_id=peer,
            device_id_type=MESH,
        )
        copy.start()
        sent[rxi, q] = copy

    def from_own(t):
        return lambda rows, cols: own.at[t, rows, cols]

    def from_rx(k):
        return lambda rows, cols: rx.at[k, rows, cols]

    def from_y(k):
        return lambda rows, cols: y.at[k, rows, cols]

    def own_blocks(t, squares):
        for q, (z, z2) in enumerate(QUADS):
            loads[t, q].wait()
            keep = mask[z, block_slot(t, z, z2) - 1].astype(F32)
            cols = pl.ds(z2 * B, B)

            def strip_step(s, total, z=z, cols=cols, keep=keep):
                rows = pl.ds(pl.multiple_of(z * B + s * 64, 64), 64)
                value = own[t, rows, cols] * keep
                own[t, rows, cols] = value
                put_split(t, rows, cols, value)
                return total + jnp.sum((value * value).reshape(8, 8, B), axis=0)

            squares = lax.fori_loop(0, 4, strip_step, squares)
        return squares

    squares = own_blocks(PR, jnp.zeros((8, B), F32))
    squares = own_blocks(ML, squares)
    pl.semaphore_wait(barrier, len(greeted))
    for q in (0, 1):
        send(from_own(PR), P_L, q, right)
        send(from_own(ML), M_R, q, left)
    squares = own_blocks(ER, squares)
    squares = own_blocks(ZD, squares)
    squares = 2.0 * squares
    trace = jnp.zeros((8, B), F32)
    diag = lax.broadcasted_iota(jnp.int32, (B, B), 0) == lax.broadcasted_iota(jnp.int32, (B, B), 1)
    for z, q in ((0, 0), (1, 3)):
        loads[DG, q].wait()
        here = pl.ds(z * B, B)
        raw = own[DG, here, here]
        value = 0.5 * (raw + raw.T) + jnp.where(diag, onsite[z : z + 1, :], 0.0)
        own[DG, here, here] = value
        put_split(DG, here, here, value)
        squares = squares + jnp.sum((value * value).reshape(32, 8, B), axis=0)
        trace = trace + jnp.sum(jnp.where(diag, value, 0.0).reshape(32, 8, B), axis=0)
    loads[DG, 1].wait()
    top, low = pl.ds(0, B), pl.ds(B, B)
    value = own[DG, top, low] * mask[0, 0].astype(F32)
    own[DG, top, low] = value
    put_split(DG, top, low, value)
    squares = squares + 2.0 * jnp.sum((value * value).reshape(32, 8, B), axis=0)
    flipped = value.T
    own[DG, low, top] = flipped
    put_split(DG, low, top, flipped)
    part[0, 0:8, :] = trace
    part[0, 8:16, :] = squares

    small = []

    def send_part(stage, peers, base):
        copies = []
        for n, peer in enumerate(peers):
            copy = pltpu.make_async_remote_copy(
                src_ref=part.at[stage],
                dst_ref=gath.at[base + n],
                send_sem=ar_send.at[base + n],
                recv_sem=ar_recv.at[base + n],
                device_id=peer,
                device_id_type=MESH,
            )
            copy.start()
            copies.append(copy)
        small.extend(copies)
        return copies

    def add_parts(stage, copies, base):
        total = part[stage]
        for n, copy in enumerate(copies):
            copy.wait_recv()
            total = total + gath[base + n]
        part[stage + 1] = total

    def prep(rxi, q, flip=False, keep=True):
        i, j = QUADS[q]

        def strip_step(s, carry):
            offset = pl.multiple_of(s * 128, 128)
            value = rx[rxi, pl.ds(i * B + offset, 128), pl.ds(j * B, B)]
            if keep:
                put_split(sp(rxi), pl.ds(i * B + offset, 128), pl.ds(j * B, B), value)
            if flip:
                put_split(sp(rxi), pl.ds(j * B, B), pl.ds(i * B + offset, 128), value.T)
            return carry

        lax.fori_loop(0, 2, strip_step, 0)

    def take(rxi, quads=range(4), forward=None, **how):
        for q in quads:
            sent[rxi, q].wait_recv()
            if forward is not None:
                send(from_rx(rxi), forward[0], q, forward[1])
            prep(rxi, q, **how)

    def take_t(rxi, quads=range(4), forward=None):
        take(rxi, quads, forward, flip=True, keep=False)

    def take_d(rxi, quads=DQUADS, forward=None):
        for q in quads:
            take(rxi, (q,), forward, flip=q == 1)

    def products(yi, terms, first=False):
        def tile(rows, cols):
            total = None if first else y[yi, rows, cols]
            for a, b, turned in terms:
                a_hi = hi[a, rows, :]
                a_lo = lo[a, rows, :]
                if turned:
                    b_hi, b_lo = hi[b, cols, :], lo[b, cols, :]
                    dims = (((1,), (1,)), ((), ()))
                else:
                    b_hi, b_lo = hi[b, :, cols], lo[b, :, cols]
                    dims = (((1,), (0,)), ((), ()))
                for u, v in ((a_hi, b_hi), (a_hi, b_lo), (a_lo, b_hi)):
                    term = lax.dot_general(u, v, dims, preferred_element_type=F32)
                    total = term if total is None else total + term
            y[yi, rows, cols] = total

        if yi == DG:
            tile(top, top)
            tile(slice(None), low)
        else:

            def column(n, carry):
                tile(slice(None), pl.ds(pl.multiple_of(n * B, B), B))
                return carry

            lax.fori_loop(0, 2, column, 0)

    outs = []

    def finish(yi, extra=None):
        quads = DQUADS if yi == DG else range(4)
        for q in quads:
            z, z2 = QUADS[q]
            if yi == DG:
                slot = 1 if q == 1 else 0
            else:
                slot = block_slot(yi, z, z2)
            if extra is not None:
                sent[extra, q].wait_recv()
            keep = mask[z, slot - 1].astype(F32) if slot else None

            def strip_step(s, carry, z=z, z2=z2, keep=keep):
                rows = pl.ds(pl.multiple_of(z * B + s * 64, 64), 64)
                cols = pl.ds(z2 * B, B)
                value = y[yi, rows, cols]
                if extra is not None:
                    value = value + rx[extra, rows, cols]
                value = value + steer[0:1, :] * (own[yi, rows, cols] - value)
                if keep is not None:
                    value = value * keep
                y[yi, rows, cols] = value
                return carry

            lax.fori_loop(0, 4, strip_step, 0)
            copy = pltpu.make_async_copy(
                y.at[yi, pl.ds(z * B, B), pl.ds(z2 * B, B)],
                out.at[z, slot],
                out_sem.at[z * 14 + slot],
            )
            copy.start()
            outs.append(copy)

    col_parts = send_part(0, col_peers, 0)

    for q in (2, 3):
        send(from_own(PR), P_L, q, right)
        send(from_own(ML), M_R, q, left)
    for q in range(4):
        send(from_own(ER), E_L, q, right)
        send(from_own(ZD), Z_R, q, left)
        send(from_own(ZD), Z_U, q, down)
        send(from_own(ER), E_W, q, up)
    for q in DQUADS:
        send(from_own(DG), D_R, q, left)
        send(from_own(DG), D_W, q, up)
    for q in range(4):
        send(from_own(PR), P_U, q, down)

    for z, slots in ((0, (2, 5, 8, 11)), (1, (1, 4, 7, 10, 13))):
        for slot in slots:
            copy = pltpu.make_async_copy(zero, out.at[z, slot], out_sem.at[z * 14 + slot])
            copy.start()
            outs.append(copy)

    for q, (i, j) in enumerate(QUADS):
        value = own[ER, pl.ds(i * B, B), pl.ds(j * B, B)].T
        put_split(ET, pl.ds(j * B, B), pl.ds(i * B, B), value)

    products(QQ, [(ET, ZD, False)], first=True)
    products(ER, [(DG, ER, False)], first=True)
    take(P_L, (0,), (P_UL, down))
    take(M_R, (0,), (M_UR, down))
    products(DG, [(DG, DG, False), (ER, ER, True), (ML, ML, True), (ZD, ZD, True), (PR, PR, True)], first=True)
    take(P_L, (1,), (P_UL, down))
    take(M_R, (1,), (M_UR, down))
    products(ML, [(DG, ML, False)], first=True)
    take(P_L, (2,), (P_UL, down))
    take(M_R, (2,), (M_UR, down))
    add_parts(0, col_parts, 0)
    row_parts = send_part(1, row_peers, 15)
    products(PR, [(DG, PR, False)], first=True)
    take_d(D_W)
    take(P_L, (3,), (P_UL, down))
    take(M_R, (3,), (M_UR, down))
    products(QQ, [(sp(M_R), sp(D_W), False)])
    for q in range(4):
        send(from_y(QQ), Q_L, q, right)

    take(E_W)
    take_t(Z_U)
    take(P_U)
    take_t(E_L, (0,), (E_WL, up))
    take(Z_R, (0,), (Z_UR, down))
    products(ZD, [(DG, ZD, False), (ZD, sp(D_W), False), (ER, sp(M_R), False), (PR, sp(E_W), True)], first=True)
    take_t(E_L, (1,), (E_WL, up))
    take(Z_R, (1,), (Z_UR, down))
    products(ER, [(ZD, sp(M_R), True), (sp(Z_U), sp(P_U), False)])
    products(PR, [(ZD, sp(E_W), False)])
    take_t(E_L, (2,), (E_WL, up))
    take(Z_R, (2,), (Z_UR, down))
    products(DG, [(sp(Z_U), sp(Z_U), True)])
    take_t(E_L, (3,), (E_WL, up))
    take(Z_R, (3,), (Z_UR, down))
    products(ZD, [(sp(E_L), sp(P_L), False)])
    products(ER, [(PR, sp(Z_R), True)])
    take_t(P_UL)
    take_t(M_UR)
    take_d(D_R, (0,), (D_WR, up))
    products(PR, [(ER, sp(Z_R), False)])
    take_d(D_R, (1,), (D_WR, up))
    products(DG, [(sp(E_L), sp(E_L), True), (sp(P_UL), sp(P_UL), True), (sp(M_UR), sp(M_UR), True)])
    take_d(D_R, (3,), (D_WR, up))
    add_parts(1, row_parts, 15)
    total = part[2]
    t1 = jnp.sum(total[0:8, :])
    t2 = jnp.sum(total[8:16, :])
    goal = float(nrow * ncol * B)
    lean = (jnp.abs(t2 - goal) - jnp.abs(2.0 * t1 - t2 - goal)) / B
    steer[...] = 2.0 / (1.0 + jnp.exp(-jnp.full((8, B), lean, F32)))
    finish(DG)
    take(Z_UR)
    products(ER, [(ER, sp(D_R), False), (sp(M_UR), sp(Z_UR), False)])
    finish(ER)
    take(E_WL)
    products(ZD, [(ML, sp(E_WL), False)])
    finish(ZD)
    products(ML, [(ZD, sp(E_WL), True)])
    take_d(D_WR)
    products(PR, [(PR, sp(D_WR), False)])
    finish(PR)
    finish(ML, Q_L)

    for copy in outs:
        copy.wait()
    for copy in small:
        copy.wait_send()
    for copy in sent.values():
        copy.wait_send()


def shards(stored_blocks, onsite, bond_mask):
    shape = stored_blocks.shape
    result = pl.pallas_call(
        kernel,
        out_shape=jax.ShapeDtypeStruct(shape[2:], F32),
        in_specs=[
            pl.BlockSpec(memory_space=pl.ANY),
            pl.BlockSpec(memory_space=pltpu.VMEM),
            pl.BlockSpec(memory_space=pltpu.SMEM),
        ],
        out_specs=pl.BlockSpec(memory_space=pl.ANY),
        scratch_shapes=[
            pltpu.VMEM((5, W2, W2), F32),
            pltpu.VMEM((NRX, W2, W2), F32),
            pltpu.VMEM((6 + NRX, W2, W2), BF16),
            pltpu.VMEM((6 + NRX, W2, W2), BF16),
            pltpu.VMEM((6, W2, W2), F32),
            pltpu.VMEM((B, B), F32),
            pltpu.VMEM((3, 16, B), F32),
            pltpu.VMEM((22, 16, B), F32),
            pltpu.VMEM((8, B), F32),
            pltpu.SemaphoreType.DMA((19,)),
            pltpu.SemaphoreType.DMA((28,)),
            pltpu.SemaphoreType.DMA((NRX * 4,)),
            pltpu.SemaphoreType.DMA((NRX * 4,)),
            pltpu.SemaphoreType.DMA((22,)),
            pltpu.SemaphoreType.DMA((22,)),
        ],
        compiler_params=pltpu.CompilerParams(
            collective_id=0, has_side_effects=True, vmem_limit_bytes=62 * 1024 * 1024
        ),
        name="sp2_step",
    )(stored_blocks[0, 0], onsite[0, 0], bond_mask[0, 0])
    return result[None, None]


def solution(mesh):
    in_specs = (
        P("row", "col", None, None, None, None),
        P("row", "col", None, None),
        P("row", "col", None, None),
    )
    out_specs = P("row", "col", None, None, None, None)
    return jax.shard_map(shards, mesh=mesh, in_specs=in_specs, out_specs=out_specs, check_vma=False)
```

```python
import jax
import jax.numpy as jnp
from jax import lax
from jax.experimental import pallas as pl
from jax.experimental.pallas import tpu as pltpu
from jax.sharding import PartitionSpec as P

MESH = pl.DeviceIdType.MESH
F32 = jnp.float32
BF16 = jnp.bfloat16
B = 256
W2 = 2 * B

DG, ER, ML, ZD, PR = range(5)
MIDDLE = {ER: 3, ML: 6, ZD: 9, PR: 12}
QQ = 5

(P_L, E_L, Q_L, M_R, Z_R, D_R, Z_U, P_U, P_UL, M_UR, Z_UR, E_W, D_W, E_WL, D_WR) = range(15)
NRX = 15
ET = 5


def sp(rx):
    return 6 + rx


QUADS = ((0, 0), (0, 1), (1, 0), (1, 1))
DQUADS = (0, 1, 3)


def block_slot(t, z, z2):
    return MIDDLE[t] + z2 - z


def kernel(stored, onsite, mask, y, own, rx, hi, lo, handed, part, gath, steer,
           in_sem, send_sem, recv_sem, ar_send, ar_recv):
    row = lax.axis_index("row")
    col = lax.axis_index("col")
    nrow = lax.axis_size("row")
    ncol = lax.axis_size("col")
    right = (row, lax.rem(col + 1, ncol))
    left = (row, lax.rem(col + ncol - 1, ncol))
    down = (lax.rem(row + 1, nrow), col)
    up = (lax.rem(row + nrow - 1, nrow), col)
    col_peers = [(row, lax.rem(col + j, ncol)) for j in range(1, ncol)]
    row_peers = [(lax.rem(row + j, nrow), col) for j in range(1, nrow)]

    loads = {}
    for t, q in [(t, q) for q in range(4) for t in (PR, ML)] + [
        (t, q) for t in (ER, ZD) for q in range(4)
    ]:
        z, z2 = QUADS[q]
        loads[t, q] = pltpu.make_async_copy(
            stored.at[z, block_slot(t, z, z2)],
            own.at[t, pl.ds(z * B, B), pl.ds(z2 * B, B)],
            in_sem.at[(t - 1) * 4 + q],
        )
    for n, (q, z, slot) in enumerate(((0, 0, 0), (1, 0, 1), (3, 1, 0))):
        i, j = QUADS[q]
        loads[DG, q] = pltpu.make_async_copy(
            stored.at[z, slot], own.at[DG, pl.ds(i * B, B), pl.ds(j * B, B)], in_sem.at[16 + n]
        )
    for copy in loads.values():
        copy.start()

    barrier = pltpu.get_barrier_semaphore()
    greeted = col_peers + row_peers
    for peer in greeted:
        pl.semaphore_signal(barrier, inc=1, device_id=peer, device_id_type=MESH)

    def put_split(k, rows, cols, value):
        high = value.astype(BF16)
        hi[k, rows, cols] = high
        lo[k, rows, cols] = (value - high.astype(F32)).astype(BF16)

    sent = {}

    def send(source, rxi, q, peer):
        i, j = QUADS[q]
        where = (pl.ds(i * B, B), pl.ds(j * B, B))
        copy = pltpu.make_async_remote_copy(
            src_ref=source(*where),
            dst_ref=rx.at[(rxi,) + where],
            send_sem=send_sem.at[rxi * 4 + q],
            recv_sem=recv_sem.at[rxi * 4 + q],
            device_id=peer,
            device_id_type=MESH,
        )
        copy.start()
        sent[rxi, q] = copy

    def from_own(t):
        return lambda rows, cols: own.at[t, rows, cols]

    def from_rx(k):
        return lambda rows, cols: rx.at[k, rows, cols]

    def from_handed(rows, cols):
        return handed.at[0, rows, cols]

    def own_block(t, q, squares):
        z, z2 = QUADS[q]
        loads[t, q].wait()
        keep = mask[z, block_slot(t, z, z2) - 1].astype(F32)
        cols = pl.ds(z2 * B, B)

        def strip_step(s, total):
            rows = pl.ds(pl.multiple_of(z * B + s * 64, 64), 64)
            value = own[t, rows, cols] * keep
            own[t, rows, cols] = value
            put_split(t, rows, cols, value)
            return total + jnp.sum((value * value).reshape(8, 8, B), axis=0)

        return lax.fori_loop(0, 4, strip_step, squares)

    squares = jnp.zeros((8, B), F32)
    for q in range(4):
        squares = own_block(PR, q, squares)
        squares = own_block(ML, q, squares)
        if q == 0:
            pl.semaphore_wait(barrier, len(greeted))
        if q < 2:
            send(from_own(PR), P_L, q, right)
            send(from_own(ML), M_R, q, left)
    for t in (ER, ZD):
        for q in range(4):
            squares = own_block(t, q, squares)
    squares = 2.0 * squares
    trace = jnp.zeros((8, B), F32)
    diag = lax.broadcasted_iota(jnp.int32, (B, B), 0) == lax.broadcasted_iota(jnp.int32, (B, B), 1)
    for z, q in ((0, 0), (1, 3)):
        loads[DG, q].wait()
        here = pl.ds(z * B, B)
        raw = own[DG, here, here]
        value = 0.5 * (raw + raw.T) + jnp.where(diag, onsite[z : z + 1, :], 0.0)
        own[DG, here, here] = value
        put_split(DG, here, here, value)
        squares = squares + jnp.sum((value * value).reshape(32, 8, B), axis=0)
        trace = trace + jnp.sum(jnp.where(diag, value, 0.0).reshape(32, 8, B), axis=0)
    loads[DG, 1].wait()
    top, low = pl.ds(0, B), pl.ds(B, B)
    value = own[DG, top, low] * mask[0, 0].astype(F32)
    own[DG, top, low] = value
    put_split(DG, top, low, value)
    squares = squares + 2.0 * jnp.sum((value * value).reshape(32, 8, B), axis=0)
    flipped = value.T
    own[DG, low, top] = flipped
    put_split(DG, low, top, flipped)
    trace = trace[:, :128] + trace[:, 128:]
    squares = squares[:, :128] + squares[:, 128:]
    part[0, 0:4, :] = trace[0:4] + trace[4:8]
    part[0, 4:8, :] = squares[0:4] + squares[4:8]

    small = []

    def send_part(stage, peers, base):
        copies = []
        for n, peer in enumerate(peers):
            copy = pltpu.make_async_remote_copy(
                src_ref=part.at[stage],
                dst_ref=gath.at[base + n],
                send_sem=ar_send.at[base + n],
                recv_sem=ar_recv.at[base + n],
                device_id=peer,
                device_id_type=MESH,
            )
            copy.start()
            copies.append(copy)
        small.extend(copies)
        return copies

    def add_parts(stage, copies, base):
        total = part[stage]
        for n, copy in enumerate(copies):
            copy.wait_recv()
            total = total + gath[base + n]
        part[stage + 1] = total

    def prep(rxi, q, flip=False, keep=True):
        i, j = QUADS[q]

        def strip_step(s, carry):
            offset = pl.multiple_of(s * 128, 128)
            value = rx[rxi, pl.ds(i * B + offset, 128), pl.ds(j * B, B)]
            if keep:
                put_split(sp(rxi), pl.ds(i * B + offset, 128), pl.ds(j * B, B), value)
            if flip:
                put_split(sp(rxi), pl.ds(j * B, B), pl.ds(i * B + offset, 128), value.T)
            return carry

        lax.fori_loop(0, 2, strip_step, 0)

    def take(rxi, quads=range(4), forward=None, **how):
        for q in quads:
            sent[rxi, q].wait_recv()
            if forward is not None:
                send(from_rx(rxi), forward[0], q, forward[1])
            prep(rxi, q, **how)

    def take_t(rxi, quads=range(4), forward=None):
        take(rxi, quads, forward, flip=True, keep=False)

    def take_d(rxi, quads=DQUADS, forward=None):
        for q in quads:
            take(rxi, (q,), forward, flip=q == 1)

    def products(yi, terms, first=False):
        held, slot = (handed, 0) if yi == QQ else (y, yi)

        def tile(rows, cols):
            total = None if first else held[slot, rows, cols]
            for a, b, turned in terms:
                a_hi = hi[a, rows, :]
                a_lo = lo[a, rows, :]
                if turned:
                    b_hi, b_lo = hi[b, cols, :], lo[b, cols, :]
                    dims = (((1,), (1,)), ((), ()))
                else:
                    b_hi, b_lo = hi[b, :, cols], lo[b, :, cols]
                    dims = (((1,), (0,)), ((), ()))
                for u, v in ((a_hi, b_hi), (a_hi, b_lo), (a_lo, b_hi)):
                    term = lax.dot_general(u, v, dims, preferred_element_type=F32)
                    total = term if total is None else total + term
            held[slot, rows, cols] = total

        if yi == DG:
            tile(top, top)
            tile(slice(None), low)
        else:

            def column(n, carry):
                tile(slice(None), pl.ds(pl.multiple_of(n * B, B), B))
                return carry

            lax.fori_loop(0, 2, column, 0)

    def finish(yi, extra=None):
        quads = DQUADS if yi == DG else range(4)
        for q in quads:
            z, z2 = QUADS[q]
            if yi == DG:
                slot = 1 if q == 1 else 0
            else:
                slot = block_slot(yi, z, z2)
            if extra is not None:
                sent[extra, q].wait_recv()
            keep = mask[z, slot - 1].astype(F32) if slot else None

            def strip_step(s, carry, z=z, z2=z2, keep=keep):
                rows = pl.ds(pl.multiple_of(z * B + s * 64, 64), 64)
                cols = pl.ds(z2 * B, B)
                value = y[yi, rows, cols]
                if extra is not None:
                    value = value + rx[extra, rows, cols]
                value = value + steer[0:1, :] * (own[yi, rows, cols] - value)
                if keep is not None:
                    value = value * keep
                y[yi, rows, cols] = value
                return carry

            lax.fori_loop(0, 4, strip_step, 0)

    col_parts = send_part(0, col_peers, 0)

    for q in (2, 3):
        send(from_own(PR), P_L, q, right)
        send(from_own(ML), M_R, q, left)
    for q in range(4):
        send(from_own(ER), E_L, q, right)
        send(from_own(ZD), Z_R, q, left)
        send(from_own(ZD), Z_U, q, down)
        send(from_own(ER), E_W, q, up)
    for q in DQUADS:
        send(from_own(DG), D_R, q, left)
        send(from_own(DG), D_W, q, up)
    for q in range(4):
        send(from_own(PR), P_U, q, down)

    for q, (i, j) in enumerate(QUADS):
        value = own[ER, pl.ds(i * B, B), pl.ds(j * B, B)].T
        put_split(ET, pl.ds(j * B, B), pl.ds(i * B, B), value)

    products(QQ, [(ET, ZD, False)], first=True)
    products(ER, [(DG, ER, False)], first=True)
    take(P_L, (0,), (P_UL, down))
    take(M_R, (0,), (M_UR, down))
    products(DG, [(DG, DG, False), (ER, ER, True), (ML, ML, True), (ZD, ZD, True), (PR, PR, True)], first=True)
    take(P_L, (1,), (P_UL, down))
    take(M_R, (1,), (M_UR, down))
    products(ML, [(DG, ML, False)], first=True)
    take(P_L, (2,), (P_UL, down))
    take(M_R, (2,), (M_UR, down))
    add_parts(0, col_parts, 0)
    row_parts = send_part(1, row_peers, 15)
    products(PR, [(DG, PR, False)], first=True)
    take_d(D_W)
    take(P_L, (3,), (P_UL, down))
    take(M_R, (3,), (M_UR, down))
    products(QQ, [(sp(M_R), sp(D_W), False)])
    for q in range(4):
        send(from_handed, Q_L, q, right)

    take(E_W)
    take_t(Z_U)
    take(P_U)
    take_t(E_L, (0,), (E_WL, up))
    take(Z_R, (0,), (Z_UR, down))
    products(ZD, [(DG, ZD, False), (ZD, sp(D_W), False), (ER, sp(M_R), False), (PR, sp(E_W), True)], first=True)
    take_t(E_L, (1,), (E_WL, up))
    take(Z_R, (1,), (Z_UR, down))
    products(ER, [(ZD, sp(M_R), True), (sp(Z_U), sp(P_U), False)])
    products(PR, [(ZD, sp(E_W), False)])
    take_t(E_L, (2,), (E_WL, up))
    take(Z_R, (2,), (Z_UR, down))
    products(DG, [(sp(Z_U), sp(Z_U), True)])
    take_t(E_L, (3,), (E_WL, up))
    take(Z_R, (3,), (Z_UR, down))
    products(ZD, [(sp(E_L), sp(P_L), False)])
    products(ER, [(PR, sp(Z_R), True)])
    take_t(P_UL)
    take_t(M_UR)
    take_d(D_R, (0,), (D_WR, up))
    products(PR, [(ER, sp(Z_R), False)])
    take_d(D_R, (1,), (D_WR, up))
    products(DG, [(sp(E_L), sp(E_L), True), (sp(P_UL), sp(P_UL), True), (sp(M_UR), sp(M_UR), True)])
    take_d(D_R, (3,), (D_WR, up))
    add_parts(1, row_parts, 15)
    total = part[2]
    t1 = jnp.sum(total[0:4, :])
    t2 = jnp.sum(total[4:8, :])
    goal = float(nrow * ncol * B)
    lean = (jnp.abs(t2 - goal) - jnp.abs(2.0 * t1 - t2 - goal)) / B
    steer[...] = 2.0 / (1.0 + jnp.exp(-jnp.full((8, B), lean, F32)))
    finish(DG)
    take(Z_UR)
    products(ER, [(ER, sp(D_R), False), (sp(M_UR), sp(Z_UR), False)])
    finish(ER)
    take(E_WL)
    products(ZD, [(ML, sp(E_WL), False)])
    finish(ZD)
    products(ML, [(ZD, sp(E_WL), True)])
    take_d(D_WR)
    products(PR, [(PR, sp(D_WR), False)])
    finish(PR)
    finish(ML, Q_L)

    for copy in small:
        copy.wait_send()
    for copy in sent.values():
        copy.wait_send()


def write(y, out, zero, sem):
    zero[...] = jnp.zeros_like(zero)
    copies = [(z, slot) for z in range(2) for slot in range(14)]
    started = []
    for t in range(5):
        for q in DQUADS if t == DG else range(4):
            z, z2 = QUADS[q]
            slot = (1 if q == 1 else 0) if t == DG else block_slot(t, z, z2)
            copies.remove((z, slot))
            started.append((y.at[t, pl.ds(z * B, B), pl.ds(z2 * B, B)], z, slot))
    started = [
        pltpu.make_async_copy(source, out.at[z, slot], sem.at[z * 14 + slot])
        for source, z, slot in started + [(zero, z, slot) for z, slot in copies]
    ]
    for copy in started:
        copy.start()
    for copy in started:
        copy.wait()


def shards(stored_blocks, onsite, bond_mask):
    squared = pl.pallas_call(
        kernel,
        out_shape=pltpu.VMEM((5, W2, W2), F32),
        in_specs=[
            pl.BlockSpec(memory_space=pltpu.HBM),
            pl.BlockSpec(memory_space=pltpu.VMEM),
            pl.BlockSpec(memory_space=pltpu.SMEM),
        ],
        out_specs=pl.BlockSpec(memory_space=pltpu.VMEM),
        scratch_shapes=[
            pltpu.VMEM((5, W2, W2), F32),
            pltpu.VMEM((NRX, W2, W2), F32),
            pltpu.VMEM((6 + NRX, W2, W2), BF16),
            pltpu.VMEM((6 + NRX, W2, W2), BF16),
            pltpu.VMEM((1, W2, W2), F32),
            pltpu.VMEM((3, 8, 128), F32),
            pltpu.VMEM((22, 8, 128), F32),
            pltpu.VMEM((8, B), F32),
            pltpu.SemaphoreType.DMA((19,)),
            pltpu.SemaphoreType.DMA((NRX * 4,)),
            pltpu.SemaphoreType.DMA((NRX * 4,)),
            pltpu.SemaphoreType.DMA((22,)),
            pltpu.SemaphoreType.DMA((22,)),
        ],
        compiler_params=pltpu.CompilerParams(
            collective_id=0, has_side_effects=True, vmem_limit_bytes=50 * 1024 * 1024
        ),
        name="sp2_step",
    )(stored_blocks[0, 0], onsite[0, 0], bond_mask[0, 0])
    result = pl.pallas_call(
        write,
        out_shape=jax.ShapeDtypeStruct(stored_blocks.shape[2:], F32),
        in_specs=[pl.BlockSpec(memory_space=pltpu.VMEM)],
        out_specs=pl.BlockSpec(memory_space=pltpu.HBM),
        scratch_shapes=[pltpu.VMEM((B, B), F32), pltpu.SemaphoreType.DMA((28,))],
        compiler_params=pltpu.CompilerParams(vmem_limit_bytes=4 * 1024 * 1024),
        name="write_out",
    )(squared)
    return result[None, None]


def solution(mesh):
    in_specs = (
        P("row", "col", None, None, None, None),
        P("row", "col", None, None),
        P("row", "col", None, None),
    )
    out_specs = P("row", "col", None, None, None, None)
    return jax.shard_map(shards, mesh=mesh, in_specs=in_specs, out_specs=out_specs, check_vma=False)
```

```python
import jax
import jax.numpy as jnp
from jax import lax
from jax.experimental import pallas as pl
from jax.experimental.pallas import tpu as pltpu
from jax.sharding import PartitionSpec as P

MESH = pl.DeviceIdType.MESH
F32 = jnp.float32
BF16 = jnp.bfloat16
B = 256
W2 = 2 * B

DG, ER, ML, ZD, PR = range(5)
MIDDLE = {ER: 3, ML: 6, ZD: 9, PR: 12}
QQ = 5

(P_L, E_L, Q_L, M_R, Z_R, D_R, Z_U, P_U, P_UL, M_UR, Z_UR, E_W, D_W, E_WL, D_WR) = range(15)
NRX = 15
ET = 5


def sp(rx):
    return 6 + rx


QUADS = ((0, 0), (0, 1), (1, 0), (1, 1))
DQUADS = (0, 1, 3)


def block_slot(t, z, z2):
    return MIDDLE[t] + z2 - z


def kernel(stored, onsite_in, mask_in, y, own, rx, hi, lo, handed, part, gath, steer, onsite, mask,
           in_sem, send_sem, recv_sem, ar_send, ar_recv, round_sem):
    row = lax.axis_index("row")
    col = lax.axis_index("col")
    nrow = lax.axis_size("row")
    ncol = lax.axis_size("col")
    right = (row, lax.rem(col + 1, ncol))
    left = (row, lax.rem(col + ncol - 1, ncol))
    down = (lax.rem(row + 1, nrow), col)
    up = (lax.rem(row + nrow - 1, nrow), col)
    col_peers = [(row, lax.rem(col + j, ncol)) for j in range(1, ncol)]
    row_peers = [(lax.rem(row + j, nrow), col) for j in range(1, nrow)]

    near = [(row, lax.rem(col + j, ncol)) for j in (1, ncol - 1, 4, ncol - 4)]
    near += [(lax.rem(row + j, nrow), col) for j in (1, nrow - 1, 2, nrow - 2)]
    barrier = pltpu.get_barrier_semaphore()

    def tell(sem):
        for peer in near:
            pl.semaphore_signal(sem, inc=1, device_id=peer, device_id_type=MESH)

    def heard(sem):
        pl.semaphore_wait(sem, len(near))

    tell(barrier)

    mask_load = pltpu.make_async_copy(mask_in, mask, in_sem.at[19])
    mask_load.start()
    loads = {}
    for t, q in [(t, q) for q in range(4) for t in (PR, ML)] + [
        (t, q) for t in (ER, ZD) for q in range(4)
    ]:
        z, z2 = QUADS[q]
        loads[t, q] = pltpu.make_async_copy(
            stored.at[z, block_slot(t, z, z2)],
            own.at[t, pl.ds(z * B, B), pl.ds(z2 * B, B)],
            in_sem.at[(t - 1) * 4 + q],
        )
    for n, (q, z, slot) in enumerate(((0, 0, 0), (1, 0, 1), (3, 1, 0))):
        i, j = QUADS[q]
        loads[DG, q] = pltpu.make_async_copy(
            stored.at[z, slot], own.at[DG, pl.ds(i * B, B), pl.ds(j * B, B)], in_sem.at[16 + n]
        )
    for copy in loads.values():
        copy.start()

    onsite_load = pltpu.make_async_copy(onsite_in, onsite, in_sem.at[20])
    onsite_load.start()
    mask_load.wait()

    def put_split(k, rows, cols, value):
        high = value.astype(BF16)
        hi[k, rows, cols] = high
        lo[k, rows, cols] = (value - high.astype(F32)).astype(BF16)

    sent = {}

    def send(source, rxi, q, peer):
        i, j = QUADS[q]
        where = (pl.ds(i * B, B), pl.ds(j * B, B))
        copy = pltpu.make_async_remote_copy(
            src_ref=source(*where),
            dst_ref=rx.at[(rxi,) + where],
            send_sem=send_sem.at[rxi * 4 + q],
            recv_sem=recv_sem.at[rxi * 4 + q],
            device_id=peer,
            device_id_type=MESH,
        )
        copy.start()
        sent[rxi, q] = copy

    def from_own(t):
        return lambda rows, cols: own.at[t, rows, cols]

    def from_rx(k):
        return lambda rows, cols: rx.at[k, rows, cols]

    def from_handed(rows, cols):
        return handed.at[0, rows, cols]

    def own_block(t, q, squares):
        z, z2 = QUADS[q]
        loads[t, q].wait()
        keep = mask[z, block_slot(t, z, z2) - 1].astype(F32)
        cols = pl.ds(z2 * B, B)

        def strip_step(s, total):
            rows = pl.ds(pl.multiple_of(z * B + s * 64, 64), 64)
            value = own[t, rows, cols] * keep
            own[t, rows, cols] = value
            put_split(t, rows, cols, value)
            return total + jnp.sum((value * value).reshape(8, 8, B), axis=0)

        return lax.fori_loop(0, 4, strip_step, squares)

    squares = own_block(PR, 0, jnp.zeros((8, B), F32))
    heard(barrier)
    send(from_own(PR), P_L, 0, right)
    tell(round_sem.at[0])
    squares = own_block(ML, 0, squares)
    send(from_own(ML), M_R, 0, left)
    squares = own_block(PR, 1, squares)
    send(from_own(PR), P_L, 1, right)
    squares = own_block(ML, 1, squares)
    send(from_own(ML), M_R, 1, left)
    for t, q in [(t, q) for q in (2, 3) for t in (PR, ML)] + [(ER, q) for q in range(4)]:
        squares = own_block(t, q, squares)
    heard(round_sem.at[0])
    tell(round_sem.at[1])
    for q in range(4):
        squares = own_block(ZD, q, squares)
    squares = 2.0 * squares
    trace = jnp.zeros((8, B), F32)
    onsite_load.wait()
    diag = lax.broadcasted_iota(jnp.int32, (B, B), 0) == lax.broadcasted_iota(jnp.int32, (B, B), 1)
    for z, q in ((0, 0), (1, 3)):
        loads[DG, q].wait()
        here = pl.ds(z * B, B)
        raw = own[DG, here, here]
        value = 0.5 * (raw + raw.T) + jnp.where(diag, onsite[z : z + 1, :], 0.0)
        own[DG, here, here] = value
        put_split(DG, here, here, value)
        squares = squares + jnp.sum((value * value).reshape(32, 8, B), axis=0)
        trace = trace + jnp.sum(jnp.where(diag, value, 0.0).reshape(32, 8, B), axis=0)
    loads[DG, 1].wait()
    top, low = pl.ds(0, B), pl.ds(B, B)
    value = own[DG, top, low] * mask[0, 0].astype(F32)
    own[DG, top, low] = value
    put_split(DG, top, low, value)
    squares = squares + 2.0 * jnp.sum((value * value).reshape(32, 8, B), axis=0)
    flipped = value.T
    own[DG, low, top] = flipped
    put_split(DG, low, top, flipped)
    trace = trace[:, :128] + trace[:, 128:]
    squares = squares[:, :128] + squares[:, 128:]
    part[0, 0:4, :] = trace[0:4] + trace[4:8]
    part[0, 4:8, :] = squares[0:4] + squares[4:8]

    small = []

    def send_part(stage, peers, base):
        copies = []
        for n, peer in enumerate(peers):
            copy = pltpu.make_async_remote_copy(
                src_ref=part.at[stage],
                dst_ref=gath.at[base + n],
                send_sem=ar_send.at[base + n],
                recv_sem=ar_recv.at[base + n],
                device_id=peer,
                device_id_type=MESH,
            )
            copy.start()
            copies.append(copy)
        small.extend(copies)
        return copies

    def add_parts(stage, copies, base):
        total = part[stage]
        for n, copy in enumerate(copies):
            copy.wait_recv()
            total = total + gath[base + n]
        part[stage + 1] = total

    def prep(rxi, q, flip=False, keep=True):
        i, j = QUADS[q]

        def strip_step(s, carry):
            offset = pl.multiple_of(s * 128, 128)
            value = rx[rxi, pl.ds(i * B + offset, 128), pl.ds(j * B, B)]
            if keep:
                put_split(sp(rxi), pl.ds(i * B + offset, 128), pl.ds(j * B, B), value)
            if flip:
                put_split(sp(rxi), pl.ds(j * B, B), pl.ds(i * B + offset, 128), value.T)
            return carry

        lax.fori_loop(0, 2, strip_step, 0)

    def take(rxi, quads=range(4), forward=None, **how):
        for q in quads:
            sent[rxi, q].wait_recv()
            if forward is not None:
                send(from_rx(rxi), forward[0], q, forward[1])
            prep(rxi, q, **how)

    def take_t(rxi, quads=range(4), forward=None):
        take(rxi, quads, forward, flip=True, keep=False)

    def take_d(rxi, quads=DQUADS, forward=None):
        for q in quads:
            take(rxi, (q,), forward, flip=q == 1)

    def products(yi, terms, first=False, column=None):
        held, slot = (handed, 0) if yi == QQ else (y, yi)

        def tile(rows, cols):
            total = None if first else held[slot, rows, cols]
            for a, b, turned in terms:
                a_hi = hi[a, rows, :]
                a_lo = lo[a, rows, :]
                if turned:
                    b_hi, b_lo = hi[b, cols, :], lo[b, cols, :]
                    dims = (((1,), (1,)), ((), ()))
                else:
                    b_hi, b_lo = hi[b, :, cols], lo[b, :, cols]
                    dims = (((1,), (0,)), ((), ()))
                for u, v in ((a_hi, b_hi), (a_hi, b_lo), (a_lo, b_hi)):
                    term = lax.dot_general(u, v, dims, preferred_element_type=F32)
                    total = term if total is None else total + term
            held[slot, rows, cols] = total

        if yi == DG:
            tile(top, top)
            tile(slice(None), low)
        elif column is not None:
            tile(slice(None), pl.ds(column * B, B))
        else:

            def each(n, carry):
                tile(slice(None), pl.ds(pl.multiple_of(n * B, B), B))
                return carry

            lax.fori_loop(0, 2, each, 0)

    def finish(yi, extra=None, quads=range(4)):
        quads = DQUADS if yi == DG else quads
        for q in quads:
            z, z2 = QUADS[q]
            if yi == DG:
                slot = 1 if q == 1 else 0
            else:
                slot = block_slot(yi, z, z2)
            if extra is not None:
                sent[extra, q].wait_recv()
            keep = mask[z, slot - 1].astype(F32) if slot else None

            def strip_step(s, carry, z=z, z2=z2, keep=keep):
                rows = pl.ds(pl.multiple_of(z * B + s * 64, 64), 64)
                cols = pl.ds(z2 * B, B)
                value = y[yi, rows, cols]
                if extra is not None:
                    value = value + rx[extra, rows, cols]
                value = value + steer[0:1, :] * (own[yi, rows, cols] - value)
                if keep is not None:
                    value = value * keep
                y[yi, rows, cols] = value
                return carry

            lax.fori_loop(0, 4, strip_step, 0)

    heard(round_sem.at[1])
    col_parts = send_part(0, col_peers, 0)

    for q in (2, 3):
        send(from_own(PR), P_L, q, right)
        send(from_own(ML), M_R, q, left)
    for q in range(4):
        send(from_own(ER), E_L, q, right)
        send(from_own(ZD), Z_R, q, left)
        send(from_own(ZD), Z_U, q, down)
        send(from_own(ER), E_W, q, up)
    for q in DQUADS:
        send(from_own(DG), D_R, q, left)
        send(from_own(DG), D_W, q, up)
    for q in range(4):
        send(from_own(PR), P_U, q, down)

    for q, (i, j) in enumerate(QUADS):
        value = own[ER, pl.ds(i * B, B), pl.ds(j * B, B)].T
        put_split(ET, pl.ds(j * B, B), pl.ds(i * B, B), value)

    products(QQ, [(ET, ZD, False)], first=True)
    products(ER, [(DG, ER, False)], first=True)
    take(P_L, (0,), (P_UL, down))
    take(M_R, (0,), (M_UR, down))
    products(DG, [(DG, DG, False), (ER, ER, True), (ML, ML, True), (ZD, ZD, True), (PR, PR, True)], first=True)
    take(P_L, (1,), (P_UL, down))
    take(M_R, (1,), (M_UR, down))
    products(ML, [(DG, ML, False)], first=True)
    take(P_L, (2,), (P_UL, down))
    take(M_R, (2,), (M_UR, down))
    add_parts(0, col_parts, 0)
    row_parts = send_part(1, row_peers, 15)
    products(PR, [(DG, PR, False)], first=True)
    take_d(D_W)
    take(P_L, (3,), (P_UL, down))
    take(M_R, (3,), (M_UR, down))
    products(QQ, [(sp(M_R), sp(D_W), False)])
    for q in range(4):
        send(from_handed, Q_L, q, right)

    take(E_W)
    take_t(Z_U)
    take(P_U)
    take_t(E_L, (0,), (E_WL, up))
    take(Z_R, (0,), (Z_UR, down))
    products(ZD, [(DG, ZD, False), (ZD, sp(D_W), False), (ER, sp(M_R), False), (PR, sp(E_W), True)], first=True)
    take_t(E_L, (1,), (E_WL, up))
    take(Z_R, (1,), (Z_UR, down))
    products(ER, [(ZD, sp(M_R), True), (sp(Z_U), sp(P_U), False)])
    products(PR, [(ZD, sp(E_W), False)])
    take_t(E_L, (2,), (E_WL, up))
    take(Z_R, (2,), (Z_UR, down))
    products(DG, [(sp(Z_U), sp(Z_U), True)])
    take_t(E_L, (3,), (E_WL, up))
    take(Z_R, (3,), (Z_UR, down))
    products(ZD, [(sp(E_L), sp(P_L), False)])
    products(ER, [(PR, sp(Z_R), True)])
    take_d(D_R, (0,), (D_WR, up))
    products(PR, [(ER, sp(Z_R), False)])
    take_t(P_UL)
    take_t(M_UR)
    products(DG, [(sp(E_L), sp(E_L), True), (sp(P_UL), sp(P_UL), True), (sp(M_UR), sp(M_UR), True)])
    add_parts(1, row_parts, 15)
    total = part[2]
    t1 = jnp.sum(total[0:4, :])
    t2 = jnp.sum(total[4:8, :])
    goal = float(nrow * ncol * B)
    lean = (jnp.abs(t2 - goal) - jnp.abs(2.0 * t1 - t2 - goal)) / B
    steer[...] = 2.0 / (1.0 + jnp.exp(-jnp.full((8, B), lean, F32)))
    take_d(D_R, (1,), (D_WR, up))
    products(ER, [(ER, sp(D_R), False)], column=0)
    finish(DG)
    take(E_WL)
    products(ZD, [(ML, sp(E_WL), False)])
    products(ML, [(ZD, sp(E_WL), True)])
    take(Z_UR)
    products(ER, [(sp(M_UR), sp(Z_UR), False)])
    finish(ZD)
    finish(ER, quads=(0, 2))
    finish(ML, Q_L, (0, 1))
    take_d(D_R, (3,), (D_WR, up))
    products(ER, [(ER, sp(D_R), False)], column=1)
    finish(ER, quads=(1, 3))
    take_d(D_WR, (0, 1))
    products(PR, [(PR, sp(D_WR), False)], column=0)
    finish(PR, quads=(0, 2))
    finish(ML, Q_L, (2,))
    take_d(D_WR, (3,))
    products(PR, [(PR, sp(D_WR), False)], column=1)
    finish(PR, quads=(1, 3))
    finish(ML, Q_L, (3,))

    for copy in small:
        copy.wait_send()
    for copy in sent.values():
        copy.wait_send()


def write(y, out, zero, sem):
    zero[...] = jnp.zeros_like(zero)
    copies = [(z, slot) for z in range(2) for slot in range(14)]
    started = []
    for t in range(5):
        for q in DQUADS if t == DG else range(4):
            z, z2 = QUADS[q]
            slot = (1 if q == 1 else 0) if t == DG else block_slot(t, z, z2)
            copies.remove((z, slot))
            started.append((y.at[t, pl.ds(z * B, B), pl.ds(z2 * B, B)], z, slot))
    started = [
        pltpu.make_async_copy(source, out.at[z, slot], sem.at[z * 14 + slot])
        for source, z, slot in started + [(zero, z, slot) for z, slot in copies]
    ]
    for copy in started:
        copy.start()
    for copy in started:
        copy.wait()


def shards(stored_blocks, onsite, bond_mask):
    squared = pl.pallas_call(
        kernel,
        out_shape=pltpu.VMEM((5, W2, W2), F32),
        in_specs=[
            pl.BlockSpec(memory_space=pltpu.HBM),
            pl.BlockSpec(memory_space=pltpu.HBM),
            pl.BlockSpec(memory_space=pltpu.HBM),
        ],
        out_specs=pl.BlockSpec(memory_space=pltpu.VMEM),
        scratch_shapes=[
            pltpu.VMEM((5, W2, W2), F32),
            pltpu.VMEM((NRX, W2, W2), F32),
            pltpu.VMEM((6 + NRX, W2, W2), BF16),
            pltpu.VMEM((6 + NRX, W2, W2), BF16),
            pltpu.VMEM((1, W2, W2), F32),
            pltpu.VMEM((3, 8, 128), F32),
            pltpu.VMEM((22, 8, 128), F32),
            pltpu.VMEM((8, B), F32),
            pltpu.VMEM((2, B), F32),
            pltpu.SMEM((2, 13), jnp.int32),
            pltpu.SemaphoreType.DMA((21,)),
            pltpu.SemaphoreType.DMA((NRX * 4,)),
            pltpu.SemaphoreType.DMA((NRX * 4,)),
            pltpu.SemaphoreType.DMA((22,)),
            pltpu.SemaphoreType.DMA((22,)),
            pltpu.SemaphoreType.REGULAR((2,)),
        ],
        compiler_params=pltpu.CompilerParams(
            collective_id=0, has_side_effects=True, vmem_limit_bytes=50 * 1024 * 1024
        ),
        name="sp2_step",
    )(stored_blocks[0, 0], onsite[0, 0], bond_mask[0, 0])
    result = pl.pallas_call(
        write,
        out_shape=jax.ShapeDtypeStruct(stored_blocks.shape[2:], F32),
        in_specs=[pl.BlockSpec(memory_space=pltpu.VMEM)],
        out_specs=pl.BlockSpec(memory_space=pltpu.HBM),
        scratch_shapes=[pltpu.VMEM((B, B), F32), pltpu.SemaphoreType.DMA((28,))],
        compiler_params=pltpu.CompilerParams(vmem_limit_bytes=4 * 1024 * 1024),
        name="write_out",
    )(squared)
    return result[None, None]


def solution(mesh):
    in_specs = (
        P("row", "col", None, None, None, None),
        P("row", "col", None, None),
        P("row", "col", None, None),
    )
    out_specs = P("row", "col", None, None, None, None)
    return jax.shard_map(shards, mesh=mesh, in_specs=in_specs, out_specs=out_specs, check_vma=False)
```

```python
import jax
import jax.numpy as jnp
from jax import lax
from jax.experimental import pallas as pl
from jax.experimental.pallas import tpu as pltpu
from jax.sharding import PartitionSpec as P

MESH = pl.DeviceIdType.MESH
F32 = jnp.float32
BF16 = jnp.bfloat16
B = 256
W2 = 2 * B

DG, ER, ML, ZD, PR = range(5)
MIDDLE = {ER: 3, ML: 6, ZD: 9, PR: 12}
DP, ZP, QQ = range(3)

(DP_L, ZP_L, Q_L, M_R, Z_R, D_R, Z_U, P_U, M_UR, Z_UR, E_W, D_W, D_WR) = range(13)
NRX = 13
ET, P_UT = 5, 6


def sp(rx):
    return 4 + rx


NSPLIT = 4 + NRX

QUADS = ((0, 0), (0, 1), (1, 0), (1, 1))
DQUADS = (0, 1, 3)
SYM = {
    0: ((0, 0, 128, 0, 256), (1, 128, 128, 128, 128)),
    1: ((2, 0, 256, 256, 256),),
    3: ((3, 256, 128, 256, 256), (4, 384, 128, 384, 128)),
}


def block_slot(t, z, z2):
    return MIDDLE[t] + z2 - z


def kernel(stored, onsite_in, mask_in, y, own, rx, hi, lo, handed, part, gath, steer, onsite, mask,
           in_sem, send_sem, recv_sem, ar_send, ar_recv, round_sem):
    row = lax.axis_index("row")
    col = lax.axis_index("col")
    nrow = lax.axis_size("row")
    ncol = lax.axis_size("col")
    right = (row, lax.rem(col + 1, ncol))
    left = (row, lax.rem(col + ncol - 1, ncol))
    down = (lax.rem(row + 1, nrow), col)
    up = (lax.rem(row + nrow - 1, nrow), col)
    col_peers = [(row, lax.rem(col + j, ncol)) for j in range(1, ncol)]
    row_peers = [(lax.rem(row + j, nrow), col) for j in range(1, nrow)]

    near = [(row, lax.rem(col + j, ncol)) for j in (1, ncol - 1, 4, ncol - 4)]
    near += [(lax.rem(row + j, nrow), col) for j in (1, nrow - 1, 2, nrow - 2)]
    barrier = pltpu.get_barrier_semaphore()

    def tell(sem):
        for peer in near:
            pl.semaphore_signal(sem, inc=1, device_id=peer, device_id_type=MESH)

    def heard(sem):
        pl.semaphore_wait(sem, len(near))

    tell(barrier)

    mask_load = pltpu.make_async_copy(mask_in, mask, in_sem.at[19])
    mask_load.start()
    loads = {}
    for t, q in [(t, q) for q in range(4) for t in (PR, ML)] + [
        (t, q) for t in (ER, ZD) for q in range(4)
    ]:
        z, z2 = QUADS[q]
        loads[t, q] = pltpu.make_async_copy(
            stored.at[z, block_slot(t, z, z2)],
            own.at[t, pl.ds(z * B, B), pl.ds(z2 * B, B)],
            in_sem.at[(t - 1) * 4 + q],
        )
    for n, (q, z, slot) in enumerate(((0, 0, 0), (1, 0, 1), (3, 1, 0))):
        i, j = QUADS[q]
        loads[DG, q] = pltpu.make_async_copy(
            stored.at[z, slot], own.at[DG, pl.ds(i * B, B), pl.ds(j * B, B)], in_sem.at[16 + n]
        )
    for copy in loads.values():
        copy.start()

    onsite_load = pltpu.make_async_copy(onsite_in, onsite, in_sem.at[20])
    onsite_load.start()
    mask_load.wait()

    def put_split(k, rows, cols, value):
        high = value.astype(BF16)
        hi[k, rows, cols] = high
        lo[k, rows, cols] = (value - high.astype(F32)).astype(BF16)

    sent = {}

    def send_piece(source, rxi, p, where, peer):
        copy = pltpu.make_async_remote_copy(
            src_ref=source(*where),
            dst_ref=rx.at[(rxi,) + where],
            send_sem=send_sem.at[rxi * 5 + p],
            recv_sem=recv_sem.at[rxi * 5 + p],
            device_id=peer,
            device_id_type=MESH,
        )
        copy.start()
        sent[rxi, p] = copy

    def send(source, rxi, q, peer):
        i, j = QUADS[q]
        send_piece(source, rxi, q, (pl.ds(i * B, B), pl.ds(j * B, B)), peer)

    def send_sym(source, rxi, q, peer):
        for p, r, nr, c, nc in SYM[q]:
            send_piece(source, rxi, p, (pl.ds(r, nr), pl.ds(c, nc)), peer)

    def arrive_sym(rxi, q, forward=None):
        for p, r, nr, c, nc in SYM[q]:
            sent[rxi, p].wait_recv()
            if forward is not None:
                send_piece(from_rx(rxi), forward[0], p, (pl.ds(r, nr), pl.ds(c, nc)), forward[1])
        if q != 1:
            o = 0 if q == 0 else B
            mirrored = rx[rxi, pl.ds(o, 128), pl.ds(o + 128, 128)].T
            rx[rxi, pl.ds(o + 128, 128), pl.ds(o, 128)] = mirrored

    def from_own(t):
        return lambda rows, cols: own.at[t, rows, cols]

    def from_rx(k):
        return lambda rows, cols: rx.at[k, rows, cols]

    def from_handed(k):
        return lambda rows, cols: handed.at[k, rows, cols]

    def own_block(t, q, squares):
        z, z2 = QUADS[q]
        loads[t, q].wait()
        keep = mask[z, block_slot(t, z, z2) - 1].astype(F32)
        cols = pl.ds(z2 * B, B)

        def strip_step(s, total):
            rows = pl.ds(pl.multiple_of(z * B + s * 64, 64), 64)
            value = own[t, rows, cols] * keep
            own[t, rows, cols] = value
            put_split(t, rows, cols, value)
            return total + jnp.sum((value * value).reshape(8, 8, B), axis=0)

        return lax.fori_loop(0, 4, strip_step, squares)

    def prep(rxi, q, flip=None, keep=True):
        i, j = QUADS[q]

        def strip_step(s, carry):
            offset = pl.multiple_of(s * 128, 128)
            value = rx[rxi, pl.ds(i * B + offset, 128), pl.ds(j * B, B)]
            if keep:
                put_split(sp(rxi), pl.ds(i * B + offset, 128), pl.ds(j * B, B), value)
            if flip is not None:
                put_split(flip, pl.ds(j * B, B), pl.ds(i * B + offset, 128), value.T)
            return carry

        lax.fori_loop(0, 2, strip_step, 0)

    def take(rxi, quads=range(4), forward=None, **how):
        for q in quads:
            sent[rxi, q].wait_recv()
            if forward is not None:
                send(from_rx(rxi), forward[0], q, forward[1])
            prep(rxi, q, **how)

    def take_t(rxi, quads=range(4), forward=None):
        take(rxi, quads, forward, flip=sp(rxi), keep=False)

    def take_d(rxi, quads=DQUADS, forward=None):
        for q in quads:
            arrive_sym(rxi, q, forward)
            prep(rxi, q, flip=sp(rxi) if q == 1 else None)

    full = slice(None)

    def products(target, slot, terms, first=False, tiles=None):
        def tile(rows, cols):
            total = None if first else target[slot, rows, cols]
            for a, b, turned in terms:
                a_hi = hi[a, rows, :]
                a_lo = lo[a, rows, :]
                if turned:
                    b_hi, b_lo = hi[b, cols, :], lo[b, cols, :]
                    dims = (((1,), (1,)), ((), ()))
                else:
                    b_hi, b_lo = hi[b, :, cols], lo[b, :, cols]
                    dims = (((1,), (0,)), ((), ()))
                for u, v in ((a_hi, b_hi), (a_hi, b_lo), (a_lo, b_hi)):
                    term = lax.dot_general(u, v, dims, preferred_element_type=F32)
                    total = term if total is None else total + term
            target[slot, rows, cols] = total

        if tiles is not None:
            for rows, cols in tiles:
                tile(rows, cols)
        else:

            def each(n, carry):
                tile(full, pl.ds(pl.multiple_of(n * B, B), B))
                return carry

            lax.fori_loop(0, 2, each, 0)

    def finish(yi, extra=None, quads=range(4)):
        quads = DQUADS if yi == DG else quads
        for q in quads:
            z, z2 = QUADS[q]
            if yi == DG:
                slot = 1 if q == 1 else 0
            else:
                slot = block_slot(yi, z, z2)
            if extra is not None and yi == DG:
                arrive_sym(extra, q)
            elif extra is not None:
                sent[extra, q].wait_recv()
            keep = mask[z, slot - 1].astype(F32) if slot else None

            def strip_step(s, carry, z=z, z2=z2, keep=keep):
                rows = pl.ds(pl.multiple_of(z * B + s * 64, 64), 64)
                cols = pl.ds(z2 * B, B)
                value = y[yi, rows, cols]
                if extra is not None:
                    value = value + rx[extra, rows, cols]
                value = value + steer[0:1, :] * (own[yi, rows, cols] - value)
                if keep is not None:
                    value = value * keep
                y[yi, rows, cols] = value
                return carry

            lax.fori_loop(0, 4, strip_step, 0)

    top, low = pl.ds(0, B), pl.ds(B, B)
    squares = own_block(PR, 0, jnp.zeros((8, B), F32))
    heard(barrier)
    send(from_own(PR), P_U, 0, down)
    tell(round_sem.at[0])
    squares = own_block(ML, 0, squares)
    send(from_own(ML), M_R, 0, left)
    squares = own_block(PR, 2, squares)
    send(from_own(PR), P_U, 2, down)
    for p, m in ((1, 1), (3, 2)):
        squares = own_block(PR, p, squares)
        send(from_own(PR), P_U, p, down)
        squares = own_block(ML, m, squares)
        send(from_own(ML), M_R, m, left)
    squares = own_block(ML, 3, squares)
    for q in range(4):
        squares = own_block(ER, q, squares)
    send(from_own(ML), M_R, 3, left)
    for q, (i, j) in enumerate(QUADS):
        send(from_own(ER), E_W, q, up)
        value = own[ER, pl.ds(i * B, B), pl.ds(j * B, B)].T
        put_split(ET, pl.ds(j * B, B), pl.ds(i * B, B), value)
    heard(round_sem.at[0])
    tell(round_sem.at[1])

    take(P_U, (0, 2), flip=P_UT)
    products(handed, DP, [(ET, ET, True), (P_UT, P_UT, True)], first=True, tiles=[(top, top)])
    send_sym(from_handed(DP), DP_L, 0, right)
    for q in range(4):
        squares = own_block(ZD, q, squares)
        send(from_own(ZD), Z_R, q, left)
        send(from_own(ZD), Z_U, q, down)
    squares = 2.0 * squares
    trace = jnp.zeros((8, B), F32)
    onsite_load.wait()
    diag = lax.broadcasted_iota(jnp.int32, (B, B), 0) == lax.broadcasted_iota(jnp.int32, (B, B), 1)
    for z, q in ((0, 0), (1, 3)):
        loads[DG, q].wait()
        here = pl.ds(z * B, B)
        raw = own[DG, here, here]
        value = 0.5 * (raw + raw.T) + jnp.where(diag, onsite[z : z + 1, :], 0.0)
        own[DG, here, here] = value
        put_split(DG, here, here, value)
        squares = squares + jnp.sum((value * value).reshape(32, 8, B), axis=0)
        trace = trace + jnp.sum(jnp.where(diag, value, 0.0).reshape(32, 8, B), axis=0)
    loads[DG, 1].wait()
    value = own[DG, top, low] * mask[0, 0].astype(F32)
    own[DG, top, low] = value
    put_split(DG, top, low, value)
    squares = squares + 2.0 * jnp.sum((value * value).reshape(32, 8, B), axis=0)
    flipped = value.T
    own[DG, low, top] = flipped
    put_split(DG, low, top, flipped)
    trace = trace[:, :128] + trace[:, 128:]
    squares = squares[:, :128] + squares[:, 128:]
    part[0, 0:4, :] = trace[0:4] + trace[4:8]
    part[0, 4:8, :] = squares[0:4] + squares[4:8]

    small = []

    def send_part(stage, peers, base):
        copies = []
        for n, peer in enumerate(peers):
            copy = pltpu.make_async_remote_copy(
                src_ref=part.at[stage],
                dst_ref=gath.at[base + n],
                send_sem=ar_send.at[base + n],
                recv_sem=ar_recv.at[base + n],
                device_id=peer,
                device_id_type=MESH,
            )
            copy.start()
            copies.append(copy)
        small.extend(copies)
        return copies

    def add_parts(stage, copies, base):
        total = part[stage]
        for n, copy in enumerate(copies):
            copy.wait_recv()
            total = total + gath[base + n]
        part[stage + 1] = total

    for q in DQUADS:
        send_sym(from_own(DG), D_W, q, up)
        send_sym(from_own(DG), D_R, q, left)

    take(P_U, (1, 3), flip=P_UT)
    products(handed, DP, [(ET, ET, True), (P_UT, P_UT, True)], first=True, tiles=[(full, low)])
    send_sym(from_handed(DP), DP_L, 1, right)
    send_sym(from_handed(DP), DP_L, 3, right)
    heard(round_sem.at[1])
    col_parts = send_part(0, col_peers, 0)

    products(handed, ZP, [(ET, PR, False)], first=True)
    take(M_R, (0, 1), (M_UR, down))
    take(E_W)
    products(handed, ZP, [(sp(M_R), sp(E_W), False)], tiles=[(top, top), (top, low)])
    for q in (0, 1):
        send(from_handed(ZP), ZP_L, q, right)
    products(y, ER, [(DG, ER, False)], first=True)
    products(y, ML, [(DG, ML, False)], first=True)
    take(M_R, (2, 3), (M_UR, down))
    products(handed, ZP, [(sp(M_R), sp(E_W), False)], tiles=[(low, top), (low, low)])
    for q in (2, 3):
        send(from_handed(ZP), ZP_L, q, right)
    products(
        y,
        DG,
        [(DG, DG, False), (ER, ER, True), (ML, ML, True), (ZD, ZD, True), (PR, PR, True)],
        first=True,
        tiles=[(top, top), (full, low)],
    )
    add_parts(0, col_parts, 0)
    row_parts = send_part(1, row_peers, 15)
    take_d(D_W)
    products(handed, QQ, [(ET, ZD, False), (sp(M_R), sp(D_W), False)], first=True)
    take(Z_R, (0,), (Z_UR, down))
    products(
        y,
        ZD,
        [(DG, ZD, False), (ZD, sp(D_W), False), (ER, sp(M_R), False), (PR, sp(E_W), True)],
        first=True,
    )
    take(Z_R, (1,), (Z_UR, down))
    products(handed, QQ, [(sp(Z_R), sp(E_W), True)], tiles=[(top, top), (top, low)])
    for q in (0, 1):
        send(from_handed(QQ), Q_L, q, right)
    take_t(Z_U)
    products(y, ER, [(ZD, sp(M_R), True), (sp(Z_U), sp(P_U), False)])
    take(Z_R, (2,), (Z_UR, down))
    products(y, PR, [(DG, PR, False), (ZD, sp(E_W), False)], first=True)
    take(Z_R, (3,), (Z_UR, down))
    products(handed, QQ, [(sp(Z_R), sp(E_W), True)], tiles=[(low, top), (low, low)])
    for q in (2, 3):
        send(from_handed(QQ), Q_L, q, right)
    take_t(M_UR)
    products(
        y,
        DG,
        [(sp(Z_U), sp(Z_U), True), (sp(M_UR), sp(M_UR), True)],
        tiles=[(top, top), (full, low)],
    )
    add_parts(1, row_parts, 15)
    total = part[2]
    t1 = jnp.sum(total[0:4, :])
    t2 = jnp.sum(total[4:8, :])
    goal = float(nrow * ncol * B)
    lean = (jnp.abs(t2 - goal) - jnp.abs(2.0 * t1 - t2 - goal)) / B
    steer[...] = 2.0 / (1.0 + jnp.exp(-jnp.full((8, B), lean, F32)))
    take_d(D_R, (0,), (D_WR, up))
    products(y, ER, [(PR, sp(Z_R), True)])
    products(y, PR, [(ER, sp(Z_R), False)])
    finish(DG, DP_L)
    finish(ZD, ZP_L)
    take_d(D_R, (1,), (D_WR, up))
    products(y, ER, [(ER, sp(D_R), False)], tiles=[(full, top)])
    take(Z_UR)
    products(y, ER, [(sp(M_UR), sp(Z_UR), False)])
    finish(ER, quads=(0, 2))
    take_d(D_R, (3,), (D_WR, up))
    products(y, ER, [(ER, sp(D_R), False)], tiles=[(full, low)])
    finish(ER, quads=(1, 3))
    finish(ML, Q_L, (0, 1))
    take_d(D_WR, (0, 1))
    products(y, PR, [(PR, sp(D_WR), False)], tiles=[(full, top)])
    finish(PR, quads=(0, 2))
    take_d(D_WR, (3,))
    products(y, PR, [(PR, sp(D_WR), False)], tiles=[(full, low)])
    finish(PR, quads=(1, 3))
    finish(ML, Q_L, (2, 3))

    for copy in small:
        copy.wait_send()
    for copy in sent.values():
        copy.wait_send()


def write(y, out, zero, sem):
    zero[...] = jnp.zeros_like(zero)
    copies = [(z, slot) for z in range(2) for slot in range(14)]
    started = []
    for t in range(5):
        for q in DQUADS if t == DG else range(4):
            z, z2 = QUADS[q]
            slot = (1 if q == 1 else 0) if t == DG else block_slot(t, z, z2)
            copies.remove((z, slot))
            started.append((y.at[t, pl.ds(z * B, B), pl.ds(z2 * B, B)], z, slot))
    started = [
        pltpu.make_async_copy(source, out.at[z, slot], sem.at[z * 14 + slot])
        for source, z, slot in started + [(zero, z, slot) for z, slot in copies]
    ]
    for copy in started:
        copy.start()
    for copy in started:
        copy.wait()


def shards(stored_blocks, onsite, bond_mask):
    squared = pl.pallas_call(
        kernel,
        out_shape=pltpu.VMEM((5, W2, W2), F32),
        in_specs=[
            pl.BlockSpec(memory_space=pltpu.HBM),
            pl.BlockSpec(memory_space=pltpu.HBM),
            pl.BlockSpec(memory_space=pltpu.HBM),
        ],
        out_specs=pl.BlockSpec(memory_space=pltpu.VMEM),
        scratch_shapes=[
            pltpu.VMEM((5, W2, W2), F32),
            pltpu.VMEM((NRX, W2, W2), F32),
            pltpu.VMEM((NSPLIT, W2, W2), BF16),
            pltpu.VMEM((NSPLIT, W2, W2), BF16),
            pltpu.VMEM((3, W2, W2), F32),
            pltpu.VMEM((3, 8, 128), F32),
            pltpu.VMEM((22, 8, 128), F32),
            pltpu.VMEM((8, B), F32),
            pltpu.VMEM((2, B), F32),
            pltpu.SMEM((2, 13), jnp.int32),
            pltpu.SemaphoreType.DMA((21,)),
            pltpu.SemaphoreType.DMA((NRX * 5,)),
            pltpu.SemaphoreType.DMA((NRX * 5,)),
            pltpu.SemaphoreType.DMA((22,)),
            pltpu.SemaphoreType.DMA((22,)),
            pltpu.SemaphoreType.REGULAR((2,)),
        ],
        compiler_params=pltpu.CompilerParams(
            collective_id=0, has_side_effects=True, vmem_limit_bytes=50 * 1024 * 1024
        ),
        name="sp2_step",
    )(stored_blocks[0, 0], onsite[0, 0], bond_mask[0, 0])
    result = pl.pallas_call(
        write,
        out_shape=jax.ShapeDtypeStruct(stored_blocks.shape[2:], F32),
        in_specs=[pl.BlockSpec(memory_space=pltpu.VMEM)],
        out_specs=pl.BlockSpec(memory_space=pltpu.HBM),
        scratch_shapes=[pltpu.VMEM((B, B), F32), pltpu.SemaphoreType.DMA((28,))],
        compiler_params=pltpu.CompilerParams(vmem_limit_bytes=4 * 1024 * 1024),
        name="write_out",
    )(squared)
    return result[None, None]


def solution(mesh):
    in_specs = (
        P("row", "col", None, None, None, None),
        P("row", "col", None, None),
        P("row", "col", None, None),
    )
    out_specs = P("row", "col", None, None, None, None)
    return jax.shard_map(shards, mesh=mesh, in_specs=in_specs, out_specs=out_specs, check_vma=False)
```

```python
import jax
import jax.numpy as jnp
from jax import lax
from jax.experimental import pallas as pl
from jax.experimental.pallas import tpu as pltpu
from jax.sharding import PartitionSpec as P

MESH = pl.DeviceIdType.MESH
F32 = jnp.float32
BF16 = jnp.bfloat16
B = 256
W2 = 2 * B

DG, ER, ML, ZD, PR = range(5)
MIDDLE = {ER: 3, ML: 6, ZD: 9, PR: 12}
DP, ZP, QQ = range(3)

(DP_L, ZP_L, Q_L, M_R, Z_R, D_R, Z_U, P_U, M_UR, Z_UR, E_W, D_W, D_WR) = range(13)
NRX = 13
ET, P_UT = 5, 6


def sp(rx):
    return 4 + rx


NSPLIT = 4 + NRX

QUADS = ((0, 0), (0, 1), (1, 0), (1, 1))
DQUADS = (0, 1, 3)
SYM = {
    0: ((0, 0, 128, 0, 256), (1, 128, 128, 128, 128)),
    1: ((2, 0, 256, 256, 256),),
    3: ((3, 256, 128, 256, 256), (4, 384, 128, 384, 128)),
}


def block_slot(t, z, z2):
    return MIDDLE[t] + z2 - z


def kernel(stored, onsite_in, mask_in, y, own, rx, hi, lo, handed, part, gath, steer, onsite, mask,
           in_sem, send_sem, recv_sem, ar_send, ar_recv, round_sem):
    row = lax.axis_index("row")
    col = lax.axis_index("col")
    nrow = lax.axis_size("row")
    ncol = lax.axis_size("col")
    right = (row, lax.rem(col + 1, ncol))
    left = (row, lax.rem(col + ncol - 1, ncol))
    down = (lax.rem(row + 1, nrow), col)
    up = (lax.rem(row + nrow - 1, nrow), col)
    col_peers = [(row, lax.rem(col + j, ncol)) for j in range(1, ncol)]
    row_peers = [(lax.rem(row + j, nrow), col) for j in range(1, nrow)]

    near = [(row, lax.rem(col + j, ncol)) for j in (1, ncol - 1, 4, ncol - 4)]
    near += [(lax.rem(row + j, nrow), col) for j in (1, nrow - 1, 2, nrow - 2)]
    barrier = pltpu.get_barrier_semaphore()

    def tell(sem):
        for peer in near:
            pl.semaphore_signal(sem, inc=1, device_id=peer, device_id_type=MESH)

    def heard(sem):
        pl.semaphore_wait(sem, len(near))

    tell(barrier)

    mask_load = pltpu.make_async_copy(mask_in, mask, in_sem.at[19])
    mask_load.start()
    loads = {}
    for t, q in [(t, q) for q in range(4) for t in (PR, ML)] + [
        (t, q) for t in (ER, ZD) for q in range(4)
    ]:
        z, z2 = QUADS[q]
        loads[t, q] = pltpu.make_async_copy(
            stored.at[z, block_slot(t, z, z2)],
            own.at[t, pl.ds(z * B, B), pl.ds(z2 * B, B)],
            in_sem.at[(t - 1) * 4 + q],
        )
    for n, (q, z, slot) in enumerate(((0, 0, 0), (1, 0, 1), (3, 1, 0))):
        i, j = QUADS[q]
        loads[DG, q] = pltpu.make_async_copy(
            stored.at[z, slot], own.at[DG, pl.ds(i * B, B), pl.ds(j * B, B)], in_sem.at[16 + n]
        )
    for copy in loads.values():
        copy.start()

    onsite_load = pltpu.make_async_copy(onsite_in, onsite, in_sem.at[20])
    onsite_load.start()
    mask_load.wait()

    def put_split(k, rows, cols, value):
        high = value.astype(BF16)
        hi[k, rows, cols] = high
        lo[k, rows, cols] = (value - high.astype(F32)).astype(BF16)

    sent = {}

    def send_piece(source, rxi, p, where, peer):
        copy = pltpu.make_async_remote_copy(
            src_ref=source(*where),
            dst_ref=rx.at[(rxi,) + where],
            send_sem=send_sem.at[rxi * 5 + p],
            recv_sem=recv_sem.at[rxi * 5 + p],
            device_id=peer,
            device_id_type=MESH,
        )
        copy.start()
        sent[rxi, p] = copy

    def send(source, rxi, q, peer):
        i, j = QUADS[q]
        send_piece(source, rxi, q, (pl.ds(i * B, B), pl.ds(j * B, B)), peer)

    def send_sym(source, rxi, q, peer):
        for p, r, nr, c, nc in SYM[q]:
            send_piece(source, rxi, p, (pl.ds(r, nr), pl.ds(c, nc)), peer)

    def arrive_sym(rxi, q, forward=None):
        for p, r, nr, c, nc in SYM[q]:
            sent[rxi, p].wait_recv()
            if forward is not None:
                send_piece(from_rx(rxi), forward[0], p, (pl.ds(r, nr), pl.ds(c, nc)), forward[1])
        if q != 1:
            o = 0 if q == 0 else B
            mirrored = rx[rxi, pl.ds(o, 128), pl.ds(o + 128, 128)].T
            rx[rxi, pl.ds(o + 128, 128), pl.ds(o, 128)] = mirrored

    def from_own(t):
        return lambda rows, cols: own.at[t, rows, cols]

    def from_rx(k):
        return lambda rows, cols: rx.at[k, rows, cols]

    def from_handed(k):
        return lambda rows, cols: handed.at[k, rows, cols]

    def own_block(t, q, squares):
        z, z2 = QUADS[q]
        loads[t, q].wait()
        keep = mask[z, block_slot(t, z, z2) - 1].astype(F32)
        cols = pl.ds(z2 * B, B)

        def strip_step(s, total):
            rows = pl.ds(pl.multiple_of(z * B + s * 64, 64), 64)
            value = own[t, rows, cols] * keep
            own[t, rows, cols] = value
            put_split(t, rows, cols, value)
            return total + jnp.sum((value * value).reshape(8, 8, B), axis=0)

        return lax.fori_loop(0, 4, strip_step, squares)

    def prep(rxi, q, flip=None, keep=True):
        i, j = QUADS[q]

        def strip_step(s, carry):
            offset = pl.multiple_of(s * 128, 128)
            value = rx[rxi, pl.ds(i * B + offset, 128), pl.ds(j * B, B)]
            if keep:
                put_split(sp(rxi), pl.ds(i * B + offset, 128), pl.ds(j * B, B), value)
            if flip is not None:
                put_split(flip, pl.ds(j * B, B), pl.ds(i * B + offset, 128), value.T)
            return carry

        lax.fori_loop(0, 2, strip_step, 0)

    def take(rxi, quads=range(4), forward=None, **how):
        for q in quads:
            sent[rxi, q].wait_recv()
            if forward is not None:
                send(from_rx(rxi), forward[0], q, forward[1])
            prep(rxi, q, **how)

    def take_t(rxi, quads=range(4), forward=None):
        take(rxi, quads, forward, flip=sp(rxi), keep=False)

    def take_d(rxi, quads=DQUADS, forward=None):
        for q in quads:
            arrive_sym(rxi, q, forward)
            prep(rxi, q, flip=sp(rxi) if q == 1 else None)

    full = slice(None)

    def products(target, slot, terms, first=False, tiles=None):
        def tile(rows, cols):
            total = None if first else target[slot, rows, cols]
            for a, b, turned in terms:
                a_hi = hi[a, rows, :]
                a_lo = lo[a, rows, :]
                if turned:
                    b_hi, b_lo = hi[b, cols, :], lo[b, cols, :]
                    dims = (((1,), (1,)), ((), ()))
                else:
                    b_hi, b_lo = hi[b, :, cols], lo[b, :, cols]
                    dims = (((1,), (0,)), ((), ()))
                for u, v in ((a_hi, b_hi), (a_hi, b_lo), (a_lo, b_hi)):
                    term = lax.dot_general(u, v, dims, preferred_element_type=F32)
                    total = term if total is None else total + term
            target[slot, rows, cols] = total

        if tiles is not None:
            for rows, cols in tiles:
                tile(rows, cols)
        else:

            def each(n, carry):
                tile(full, pl.ds(pl.multiple_of(n * B, B), B))
                return carry

            lax.fori_loop(0, 2, each, 0)

    def finish(yi, extra=None, quads=range(4)):
        quads = DQUADS if yi == DG else quads
        for q in quads:
            z, z2 = QUADS[q]
            if yi == DG:
                slot = 1 if q == 1 else 0
            else:
                slot = block_slot(yi, z, z2)
            if extra is not None and yi == DG:
                arrive_sym(extra, q)
            elif extra is not None:
                sent[extra, q].wait_recv()
            keep = mask[z, slot - 1].astype(F32) if slot else None

            def strip_step(s, carry, z=z, z2=z2, keep=keep):
                rows = pl.ds(pl.multiple_of(z * B + s * 64, 64), 64)
                cols = pl.ds(z2 * B, B)
                value = y[yi, rows, cols]
                if extra is not None:
                    value = value + rx[extra, rows, cols]
                value = value + steer[0:1, :] * (own[yi, rows, cols] - value)
                if keep is not None:
                    value = value * keep
                y[yi, rows, cols] = value
                return carry

            lax.fori_loop(0, 4, strip_step, 0)

    top, low = pl.ds(0, B), pl.ds(B, B)
    squares = own_block(PR, 0, jnp.zeros((8, B), F32))
    heard(barrier)
    send(from_own(PR), P_U, 0, down)
    tell(round_sem.at[0])
    squares = own_block(ML, 0, squares)
    send(from_own(ML), M_R, 0, left)
    squares = own_block(PR, 2, squares)
    send(from_own(PR), P_U, 2, down)
    squares = own_block(PR, 1, squares)
    send(from_own(PR), P_U, 1, down)
    squares = own_block(ML, 1, squares)
    send(from_own(ML), M_R, 1, left)
    squares = own_block(PR, 3, squares)
    send(from_own(PR), P_U, 3, down)
    for q in (2, 3):
        squares = own_block(ML, q, squares)
    for q in range(4):
        squares = own_block(ER, q, squares)
    for q, (i, j) in enumerate(QUADS):
        send(from_own(ER), E_W, q, up)
        value = own[ER, pl.ds(i * B, B), pl.ds(j * B, B)].T
        put_split(ET, pl.ds(j * B, B), pl.ds(i * B, B), value)
    heard(round_sem.at[0])
    tell(round_sem.at[1])

    take(P_U, (0, 2), flip=P_UT)
    products(handed, DP, [(ET, ET, True), (P_UT, P_UT, True)], first=True, tiles=[(top, top)])
    send_sym(from_handed(DP), DP_L, 0, right)
    for q in range(4):
        squares = own_block(ZD, q, squares)
        send(from_own(ZD), Z_U, q, down)
    squares = 2.0 * squares
    trace = jnp.zeros((8, B), F32)
    onsite_load.wait()
    diag = lax.broadcasted_iota(jnp.int32, (B, B), 0) == lax.broadcasted_iota(jnp.int32, (B, B), 1)
    for z, q in ((0, 0), (1, 3)):
        loads[DG, q].wait()
        here = pl.ds(z * B, B)
        raw = own[DG, here, here]
        value = 0.5 * (raw + raw.T) + jnp.where(diag, onsite[z : z + 1, :], 0.0)
        own[DG, here, here] = value
        put_split(DG, here, here, value)
        squares = squares + jnp.sum((value * value).reshape(32, 8, B), axis=0)
        trace = trace + jnp.sum(jnp.where(diag, value, 0.0).reshape(32, 8, B), axis=0)
    loads[DG, 1].wait()
    value = own[DG, top, low] * mask[0, 0].astype(F32)
    own[DG, top, low] = value
    put_split(DG, top, low, value)
    squares = squares + 2.0 * jnp.sum((value * value).reshape(32, 8, B), axis=0)
    flipped = value.T
    own[DG, low, top] = flipped
    put_split(DG, low, top, flipped)
    trace = trace[:, :128] + trace[:, 128:]
    squares = squares[:, :128] + squares[:, 128:]
    part[0, 0:4, :] = trace[0:4] + trace[4:8]
    part[0, 4:8, :] = squares[0:4] + squares[4:8]

    small = []

    def send_part(stage, peers, base):
        copies = []
        for n, peer in enumerate(peers):
            copy = pltpu.make_async_remote_copy(
                src_ref=part.at[stage],
                dst_ref=gath.at[base + n],
                send_sem=ar_send.at[base + n],
                recv_sem=ar_recv.at[base + n],
                device_id=peer,
                device_id_type=MESH,
            )
            copy.start()
            copies.append(copy)
        small.extend(copies)
        return copies

    def add_parts(stage, copies, base):
        total = part[stage]
        for n, copy in enumerate(copies):
            copy.wait_recv()
            total = total + gath[base + n]
        part[stage + 1] = total

    heard(round_sem.at[1])
    col_parts = send_part(0, col_peers, 0)
    for q in (2, 3):
        send(from_own(ML), M_R, q, left)
    for q in range(4):
        send(from_own(ZD), Z_R, q, left)
    for q in DQUADS:
        send_sym(from_own(DG), D_W, q, up)
        send_sym(from_own(DG), D_R, q, left)

    take(P_U, (1, 3), flip=P_UT)
    products(handed, DP, [(ET, ET, True), (P_UT, P_UT, True)], first=True, tiles=[(full, low)])
    send_sym(from_handed(DP), DP_L, 1, right)
    send_sym(from_handed(DP), DP_L, 3, right)

    products(handed, ZP, [(ET, PR, False)], first=True)
    take(M_R, (0, 1), (M_UR, down))
    take(E_W)
    products(handed, ZP, [(sp(M_R), sp(E_W), False)], tiles=[(top, top), (top, low)])
    for q in (0, 1):
        send(from_handed(ZP), ZP_L, q, right)
    products(y, ER, [(DG, ER, False)], first=True)
    products(y, ML, [(DG, ML, False)], first=True)
    take(M_R, (2, 3), (M_UR, down))
    products(handed, ZP, [(sp(M_R), sp(E_W), False)], tiles=[(low, top), (low, low)])
    for q in (2, 3):
        send(from_handed(ZP), ZP_L, q, right)
    products(
        y,
        DG,
        [(DG, DG, False), (ER, ER, True), (ML, ML, True), (ZD, ZD, True), (PR, PR, True)],
        first=True,
        tiles=[(top, top), (full, low)],
    )
    add_parts(0, col_parts, 0)
    row_parts = send_part(1, row_peers, 15)
    take_d(D_W)
    products(handed, QQ, [(ET, ZD, False), (sp(M_R), sp(D_W), False)], first=True)
    take(Z_R, (0,), (Z_UR, down))
    products(
        y,
        ZD,
        [(DG, ZD, False), (ZD, sp(D_W), False), (ER, sp(M_R), False), (PR, sp(E_W), True)],
        first=True,
    )
    take(Z_R, (1,), (Z_UR, down))
    products(handed, QQ, [(sp(Z_R), sp(E_W), True)], tiles=[(top, top), (top, low)])
    for q in (0, 1):
        send(from_handed(QQ), Q_L, q, right)
    take_t(Z_U)
    products(y, ER, [(ZD, sp(M_R), True), (sp(Z_U), sp(P_U), False)])
    take(Z_R, (2,), (Z_UR, down))
    products(y, PR, [(DG, PR, False), (ZD, sp(E_W), False)], first=True)
    take(Z_R, (3,), (Z_UR, down))
    products(handed, QQ, [(sp(Z_R), sp(E_W), True)], tiles=[(low, top), (low, low)])
    for q in (2, 3):
        send(from_handed(QQ), Q_L, q, right)
    take_t(M_UR)
    products(
        y,
        DG,
        [(sp(Z_U), sp(Z_U), True), (sp(M_UR), sp(M_UR), True)],
        tiles=[(top, top), (full, low)],
    )
    add_parts(1, row_parts, 15)
    total = part[2]
    t1 = jnp.sum(total[0:4, :])
    t2 = jnp.sum(total[4:8, :])
    goal = float(nrow * ncol * B)
    lean = (jnp.abs(t2 - goal) - jnp.abs(2.0 * t1 - t2 - goal)) / B
    steer[...] = 2.0 / (1.0 + jnp.exp(-jnp.full((8, B), lean, F32)))
    take_d(D_R, (0,), (D_WR, up))
    products(y, ER, [(PR, sp(Z_R), True)])
    products(y, PR, [(ER, sp(Z_R), False)])
    finish(DG, DP_L)
    finish(ZD, ZP_L)
    take_d(D_R, (1,), (D_WR, up))
    products(y, ER, [(ER, sp(D_R), False)], tiles=[(full, top)])
    take(Z_UR)
    products(y, ER, [(sp(M_UR), sp(Z_UR), False)])
    finish(ER, quads=(0, 2))
    take_d(D_R, (3,), (D_WR, up))
    products(y, ER, [(ER, sp(D_R), False)], tiles=[(full, low)])
    finish(ER, quads=(1, 3))
    finish(ML, Q_L, (0, 1))
    take_d(D_WR, (0, 1))
    products(y, PR, [(PR, sp(D_WR), False)], tiles=[(full, top)])
    finish(PR, quads=(0, 2))
    take_d(D_WR, (3,))
    products(y, PR, [(PR, sp(D_WR), False)], tiles=[(full, low)])
    finish(PR, quads=(1, 3))
    finish(ML, Q_L, (2, 3))

    for copy in small:
        copy.wait_send()
    for copy in sent.values():
        copy.wait_send()


def write(y, out, zero, sem):
    zero[...] = jnp.zeros_like(zero)
    copies = [(z, slot) for z in range(2) for slot in range(14)]
    started = []
    for t in range(5):
        for q in DQUADS if t == DG else range(4):
            z, z2 = QUADS[q]
            slot = (1 if q == 1 else 0) if t == DG else block_slot(t, z, z2)
            copies.remove((z, slot))
            started.append((y.at[t, pl.ds(z * B, B), pl.ds(z2 * B, B)], z, slot))
    started = [
        pltpu.make_async_copy(source, out.at[z, slot], sem.at[z * 14 + slot])
        for source, z, slot in started + [(zero, z, slot) for z, slot in copies]
    ]
    for copy in started:
        copy.start()
    for copy in started:
        copy.wait()


def shards(stored_blocks, onsite, bond_mask):
    squared = pl.pallas_call(
        kernel,
        out_shape=pltpu.VMEM((5, W2, W2), F32),
        in_specs=[
            pl.BlockSpec(memory_space=pltpu.HBM),
            pl.BlockSpec(memory_space=pltpu.HBM),
            pl.BlockSpec(memory_space=pltpu.HBM),
        ],
        out_specs=pl.BlockSpec(memory_space=pltpu.VMEM),
        scratch_shapes=[
            pltpu.VMEM((5, W2, W2), F32),
            pltpu.VMEM((NRX, W2, W2), F32),
            pltpu.VMEM((NSPLIT, W2, W2), BF16),
            pltpu.VMEM((NSPLIT, W2, W2), BF16),
            pltpu.VMEM((3, W2, W2), F32),
            pltpu.VMEM((3, 8, 128), F32),
            pltpu.VMEM((22, 8, 128), F32),
            pltpu.VMEM((8, B), F32),
            pltpu.VMEM((2, B), F32),
            pltpu.SMEM((2, 13), jnp.int32),
            pltpu.SemaphoreType.DMA((21,)),
            pltpu.SemaphoreType.DMA((NRX * 5,)),
            pltpu.SemaphoreType.DMA((NRX * 5,)),
            pltpu.SemaphoreType.DMA((22,)),
            pltpu.SemaphoreType.DMA((22,)),
            pltpu.SemaphoreType.REGULAR((2,)),
        ],
        compiler_params=pltpu.CompilerParams(
            collective_id=0, has_side_effects=True, vmem_limit_bytes=50 * 1024 * 1024
        ),
        name="sp2_step",
    )(stored_blocks[0, 0], onsite[0, 0], bond_mask[0, 0])
    result = pl.pallas_call(
        write,
        out_shape=jax.ShapeDtypeStruct(stored_blocks.shape[2:], F32),
        in_specs=[pl.BlockSpec(memory_space=pltpu.VMEM)],
        out_specs=pl.BlockSpec(memory_space=pltpu.HBM),
        scratch_shapes=[pltpu.VMEM((B, B), F32), pltpu.SemaphoreType.DMA((28,))],
        compiler_params=pltpu.CompilerParams(vmem_limit_bytes=4 * 1024 * 1024),
        name="write_out",
    )(squared)
    return result[None, None]


def solution(mesh):
    in_specs = (
        P("row", "col", None, None, None, None),
        P("row", "col", None, None),
        P("row", "col", None, None),
    )
    out_specs = P("row", "col", None, None, None, None)
    return jax.shard_map(shards, mesh=mesh, in_specs=in_specs, out_specs=out_specs, check_vma=False)
```

```python
import jax
import jax.numpy as jnp
from jax import lax
from jax.experimental import pallas as pl
from jax.experimental.pallas import tpu as pltpu
from jax.sharding import PartitionSpec as P

MESH = pl.DeviceIdType.MESH
F32 = jnp.float32
BF16 = jnp.bfloat16
B = 256
W2 = 2 * B

DG, ER, ML, ZD, PR = range(5)
MIDDLE = {ER: 3, ML: 6, ZD: 9, PR: 12}
DP, ZP, QQ = range(3)

(DP_L, ZP_L, Q_L, M_R, Z_R, D_R, Z_U, P_U, M_UR, Z_UR, E_W, D_W, D_WR) = range(13)
NRX = 13
ET, P_UT = 5, 6


def sp(rx):
    return 4 + rx


NSPLIT = 4 + NRX

QUADS = ((0, 0), (0, 1), (1, 0), (1, 1))
DQUADS = (0, 1, 3)
SYM = {
    0: ((0, 0, 128, 0, 256), (1, 128, 128, 128, 128)),
    1: ((2, 0, 256, 256, 256),),
    3: ((3, 256, 128, 256, 256), (4, 384, 128, 384, 128)),
}


def block_slot(t, z, z2):
    return MIDDLE[t] + z2 - z


def kernel(stored, onsite_in, mask_in, y, own, rx, hi, lo, handed, part, gath, steer, onsite, mask,
           in_sem, send_sem, recv_sem, ar_send, ar_recv, round_sem):
    row = lax.axis_index("row")
    col = lax.axis_index("col")
    nrow = lax.axis_size("row")
    ncol = lax.axis_size("col")
    right = (row, lax.rem(col + 1, ncol))
    left = (row, lax.rem(col + ncol - 1, ncol))
    down = (lax.rem(row + 1, nrow), col)
    up = (lax.rem(row + nrow - 1, nrow), col)
    col_peers = [(row, lax.rem(col + j, ncol)) for j in range(1, ncol)]
    row_peers = [(lax.rem(row + j, nrow), col) for j in range(1, nrow)]

    near = [(row, lax.rem(col + j, ncol)) for j in (1, ncol - 1, 4, ncol - 4)]
    near += [(lax.rem(row + j, nrow), col) for j in (1, nrow - 1, 2, nrow - 2)]
    barrier = pltpu.get_barrier_semaphore()

    def tell(sem):
        for peer in near:
            pl.semaphore_signal(sem, inc=1, device_id=peer, device_id_type=MESH)

    def heard(sem):
        pl.semaphore_wait(sem, len(near))

    tell(barrier)

    mask_load = pltpu.make_async_copy(mask_in, mask, in_sem.at[19])
    mask_load.start()
    loads = {}
    for t, q in [(t, q) for q in (0, 2, 1, 3) for t in (PR, ML, ER)] + [(ZD, q) for q in range(4)]:
        z, z2 = QUADS[q]
        loads[t, q] = pltpu.make_async_copy(
            stored.at[z, block_slot(t, z, z2)],
            own.at[t, pl.ds(z * B, B), pl.ds(z2 * B, B)],
            in_sem.at[(t - 1) * 4 + q],
        )
    for n, (q, z, slot) in enumerate(((0, 0, 0), (1, 0, 1), (3, 1, 0))):
        i, j = QUADS[q]
        loads[DG, q] = pltpu.make_async_copy(
            stored.at[z, slot], own.at[DG, pl.ds(i * B, B), pl.ds(j * B, B)], in_sem.at[16 + n]
        )
    for copy in loads.values():
        copy.start()

    onsite_load = pltpu.make_async_copy(onsite_in, onsite, in_sem.at[20])
    onsite_load.start()
    mask_load.wait()

    def put_split(k, rows, cols, value):
        high = value.astype(BF16)
        hi[k, rows, cols] = high
        lo[k, rows, cols] = (value - high.astype(F32)).astype(BF16)

    sent = {}

    def send_piece(source, rxi, p, where, peer, start=True):
        copy = pltpu.make_async_remote_copy(
            src_ref=source(*where),
            dst_ref=rx.at[(rxi,) + where],
            send_sem=send_sem.at[rxi * 5 + p],
            recv_sem=recv_sem.at[rxi * 5 + p],
            device_id=peer,
            device_id_type=MESH,
        )
        if start:
            copy.start()
        sent[rxi, p] = copy

    def send(source, rxi, q, peer):
        i, j = QUADS[q]
        send_piece(source, rxi, q, (pl.ds(i * B, B), pl.ds(j * B, B)), peer)

    def send_sym(source, rxi, q, peer, start=True):
        for p, r, nr, c, nc in SYM[q]:
            send_piece(source, rxi, p, (pl.ds(r, nr), pl.ds(c, nc)), peer, start)

    def arrive_sym(rxi, q, forward=None):
        for p, r, nr, c, nc in SYM[q]:
            sent[rxi, p].wait_recv()
            if forward is not None:
                send_piece(from_rx(rxi), forward[0], p, (pl.ds(r, nr), pl.ds(c, nc)), forward[1])
        if q != 1:
            o = 0 if q == 0 else B
            mirrored = rx[rxi, pl.ds(o, 128), pl.ds(o + 128, 128)].T
            rx[rxi, pl.ds(o + 128, 128), pl.ds(o, 128)] = mirrored

    def from_own(t):
        return lambda rows, cols: own.at[t, rows, cols]

    def from_rx(k):
        return lambda rows, cols: rx.at[k, rows, cols]

    def from_handed(k):
        return lambda rows, cols: handed.at[k, rows, cols]

    def own_block(t, q, squares):
        z, z2 = QUADS[q]
        loads[t, q].wait()
        keep = mask[z, block_slot(t, z, z2) - 1].astype(F32)
        cols = pl.ds(z2 * B, B)

        def strip_step(s, total):
            rows = pl.ds(pl.multiple_of(z * B + s * 64, 64), 64)
            value = own[t, rows, cols] * keep
            own[t, rows, cols] = value
            put_split(t, rows, cols, value)
            return total + jnp.sum((value * value).reshape(8, 8, B), axis=0)

        return lax.fori_loop(0, 4, strip_step, squares, unroll=True)

    def prep(rxi, q, flip=None, keep=True):
        i, j = QUADS[q]

        def strip_step(s, carry):
            offset = pl.multiple_of(s * 128, 128)
            value = rx[rxi, pl.ds(i * B + offset, 128), pl.ds(j * B, B)]
            if keep:
                put_split(sp(rxi), pl.ds(i * B + offset, 128), pl.ds(j * B, B), value)
            if flip is not None:
                put_split(flip, pl.ds(j * B, B), pl.ds(i * B + offset, 128), value.T)
            return carry

        lax.fori_loop(0, 2, strip_step, 0)

    def take(rxi, quads=range(4), forward=None, **how):
        for q in quads:
            sent[rxi, q].wait_recv()
            if forward is not None:
                send(from_rx(rxi), forward[0], q, forward[1])
            prep(rxi, q, **how)

    def take_t(rxi, quads=range(4), forward=None):
        take(rxi, quads, forward, flip=sp(rxi), keep=False)

    def take_d(rxi, quads=DQUADS, forward=None):
        for q in quads:
            arrive_sym(rxi, q, forward)
            prep(rxi, q, flip=sp(rxi) if q == 1 else None)

    full = slice(None)

    def products(target, slot, terms, first=False, tiles=None):
        def tile(rows, cols):
            total = None if first else target[slot, rows, cols]
            for a, b, turned in terms:
                a_hi = hi[a, rows, :]
                a_lo = lo[a, rows, :]
                if turned:
                    b_hi, b_lo = hi[b, cols, :], lo[b, cols, :]
                    dims = (((1,), (1,)), ((), ()))
                else:
                    b_hi, b_lo = hi[b, :, cols], lo[b, :, cols]
                    dims = (((1,), (0,)), ((), ()))
                for u, v in ((a_hi, b_hi), (a_hi, b_lo), (a_lo, b_hi)):
                    term = lax.dot_general(u, v, dims, preferred_element_type=F32)
                    total = term if total is None else total + term
            target[slot, rows, cols] = total

        if tiles is not None:
            for rows, cols in tiles:
                tile(rows, cols)
        else:

            def each(n, carry):
                tile(full, pl.ds(pl.multiple_of(n * B, B), B))
                return carry

            lax.fori_loop(0, 2, each, 0)

    def finish(yi, extra=None, quads=range(4)):
        quads = DQUADS if yi == DG else quads
        for q in quads:
            z, z2 = QUADS[q]
            if yi == DG:
                slot = 1 if q == 1 else 0
            else:
                slot = block_slot(yi, z, z2)
            if extra is not None and yi == DG:
                arrive_sym(extra, q)
            elif extra is not None:
                sent[extra, q].wait_recv()
            keep = mask[z, slot - 1].astype(F32) if slot else None

            def strip_step(s, carry, z=z, z2=z2, keep=keep):
                rows = pl.ds(pl.multiple_of(z * B + s * 64, 64), 64)
                cols = pl.ds(z2 * B, B)
                value = y[yi, rows, cols]
                if extra is not None:
                    value = value + rx[extra, rows, cols]
                value = value + steer[0:1, :] * (own[yi, rows, cols] - value)
                if keep is not None:
                    value = value * keep
                y[yi, rows, cols] = value
                return carry

            lax.fori_loop(0, 4, strip_step, 0, unroll=True)

    top, low = pl.ds(0, B), pl.ds(B, B)
    def turn_own(quads):
        for q in quads:
            i, j = QUADS[q]
            value = own[ER, pl.ds(i * B, B), pl.ds(j * B, B)].T
            put_split(ET, pl.ds(j * B, B), pl.ds(i * B, B), value)

    squares = own_block(PR, 0, jnp.zeros((8, B), F32))
    heard(barrier)
    send(from_own(PR), P_U, 0, down)
    tell(round_sem.at[0])
    squares = own_block(ML, 0, squares)
    send(from_own(ML), M_R, 0, left)
    squares = own_block(ER, 0, squares)
    send(from_own(ER), E_W, 0, up)
    squares = own_block(PR, 2, squares)
    send(from_own(PR), P_U, 2, down)
    squares = own_block(ER, 2, squares)
    send(from_own(ER), E_W, 2, up)
    turn_own((0, 2))
    squares = own_block(PR, 1, squares)
    send(from_own(PR), P_U, 1, down)
    send_sym(from_handed(DP), DP_L, 0, right, start=False)
    diagonal_sums = [(ET, ET, True), (P_UT, P_UT, True)]

    def start_of_diagonal():
        take(P_U, (0, 2), flip=P_UT)
        products(handed, DP, diagonal_sums, first=True, tiles=[(top, top)])
        for p in (0, 1):
            sent[DP_L, p].start()

    pl.when(lax.rem(row, 2) == 1)(start_of_diagonal)
    squares = own_block(PR, 3, squares)
    send(from_own(PR), P_U, 3, down)
    for q in (1, 3):
        squares = own_block(ER, q, squares)
        send(from_own(ER), E_W, q, up)
    squares = own_block(ML, 1, squares)
    send(from_own(ML), M_R, 1, left)
    heard(round_sem.at[0])
    tell(round_sem.at[1])
    pl.when(lax.rem(row, 2) == 0)(start_of_diagonal)
    turn_own((1, 3))
    for q in (1, 3):
        send_sym(from_handed(DP), DP_L, q, right, start=False)

    def rest_of_diagonal():
        take(P_U, (1, 3), flip=P_UT)
        products(handed, DP, diagonal_sums, first=True, tiles=[(full, low)])
        for p in (2, 3, 4):
            sent[DP_L, p].start()

    pl.when(lax.rem(row, 2) == 1)(rest_of_diagonal)
    for q in (2, 3):
        squares = own_block(ML, q, squares)
    send(from_own(ML), M_R, 2, left)
    for q in range(4):
        squares = own_block(ZD, q, squares)
        send(from_own(ZD), Z_U, q, down)
    squares = 2.0 * squares
    trace = jnp.zeros((8, B), F32)
    onsite_load.wait()
    diag = lax.broadcasted_iota(jnp.int32, (B, B), 0) == lax.broadcasted_iota(jnp.int32, (B, B), 1)
    for z, q in ((0, 0), (1, 3)):
        loads[DG, q].wait()
        here = pl.ds(z * B, B)
        raw = own[DG, here, here]
        value = 0.5 * (raw + raw.T) + jnp.where(diag, onsite[z : z + 1, :], 0.0)
        own[DG, here, here] = value
        put_split(DG, here, here, value)
        squares = squares + jnp.sum((value * value).reshape(32, 8, B), axis=0)
        trace = trace + jnp.sum(jnp.where(diag, value, 0.0).reshape(32, 8, B), axis=0)
    loads[DG, 1].wait()
    value = own[DG, top, low] * mask[0, 0].astype(F32)
    own[DG, top, low] = value
    put_split(DG, top, low, value)
    squares = squares + 2.0 * jnp.sum((value * value).reshape(32, 8, B), axis=0)
    flipped = value.T
    own[DG, low, top] = flipped
    put_split(DG, low, top, flipped)
    trace = trace[:, :128] + trace[:, 128:]
    squares = squares[:, :128] + squares[:, 128:]
    part[0, 0:1, :] = jnp.sum(trace, axis=0, keepdims=True)
    part[0, 1:2, :] = jnp.sum(squares, axis=0, keepdims=True)

    small = []

    def send_part(stage, peers, base):
        copies = []
        for n, peer in enumerate(peers):
            copy = pltpu.make_async_remote_copy(
                src_ref=part.at[stage],
                dst_ref=gath.at[base + n],
                send_sem=ar_send.at[base + n],
                recv_sem=ar_recv.at[base + n],
                device_id=peer,
                device_id_type=MESH,
            )
            copy.start()
            copies.append(copy)
        small.extend(copies)
        return copies

    def add_parts(stage, copies, base):
        total = part[stage]
        for n, copy in enumerate(copies):
            copy.wait_recv()
            total = total + gath[base + n]
        part[stage + 1] = total

    heard(round_sem.at[1])
    col_parts = send_part(0, col_peers, 0)
    send(from_own(ML), M_R, 3, left)
    for q in range(4):
        send(from_own(ZD), Z_R, q, left)
    for q in DQUADS:
        send_sym(from_own(DG), D_W, q, up)
        send_sym(from_own(DG), D_R, q, left)

    pl.when(lax.rem(row, 2) == 0)(rest_of_diagonal)

    products(handed, ZP, [(ET, PR, False)], first=True)
    take(M_R, (0, 1), (M_UR, down))
    take(E_W, (0, 2, 1, 3))
    products(handed, ZP, [(sp(M_R), sp(E_W), False)], tiles=[(top, top), (top, low)])
    for q in (0, 1):
        send(from_handed(ZP), ZP_L, q, right)
    products(y, ER, [(DG, ER, False)], first=True)
    products(y, ML, [(DG, ML, False)], first=True)
    take(M_R, (2, 3), (M_UR, down))
    products(handed, ZP, [(sp(M_R), sp(E_W), False)], tiles=[(low, top), (low, low)])
    for q in (2, 3):
        send(from_handed(ZP), ZP_L, q, right)
    products(
        y,
        DG,
        [(DG, DG, False), (ER, ER, True), (ML, ML, True), (ZD, ZD, True), (PR, PR, True)],
        first=True,
        tiles=[(top, top), (full, low)],
    )
    add_parts(0, col_parts, 0)
    row_parts = send_part(1, row_peers, 15)
    take_d(D_W)
    products(handed, QQ, [(ET, ZD, False), (sp(M_R), sp(D_W), False)], first=True)
    products(y, PR, [(DG, PR, False), (ZD, sp(E_W), False)], first=True)
    take(Z_R, (0, 1), (Z_UR, down))
    products(handed, QQ, [(sp(Z_R), sp(E_W), True)], tiles=[(top, top), (top, low)])
    for q in (0, 1):
        send(from_handed(QQ), Q_L, q, right)
    products(
        y,
        ZD,
        [(DG, ZD, False), (ZD, sp(D_W), False), (ER, sp(M_R), False), (PR, sp(E_W), True)],
        first=True,
    )
    take(Z_R, (2,), (Z_UR, down))
    take_t(Z_U)
    products(y, ER, [(ZD, sp(M_R), True), (sp(Z_U), sp(P_U), False)])
    take(Z_R, (3,), (Z_UR, down))
    products(handed, QQ, [(sp(Z_R), sp(E_W), True)], tiles=[(low, top), (low, low)])
    for q in (2, 3):
        send(from_handed(QQ), Q_L, q, right)
    take_t(M_UR)
    products(
        y,
        DG,
        [(sp(Z_U), sp(Z_U), True), (sp(M_UR), sp(M_UR), True)],
        tiles=[(top, top), (full, low)],
    )
    add_parts(1, row_parts, 15)
    total = part[2]
    t1 = jnp.sum(total[0:1, :])
    t2 = jnp.sum(total[1:2, :])
    goal = float(nrow * ncol * B)
    lean = (jnp.abs(t2 - goal) - jnp.abs(2.0 * t1 - t2 - goal)) / B
    steer[...] = 2.0 / (1.0 + jnp.exp(-jnp.full((8, B), lean, F32)))
    take_d(D_R, (0,), (D_WR, up))
    products(y, ER, [(PR, sp(Z_R), True)])
    products(y, PR, [(ER, sp(Z_R), False)])
    finish(DG, DP_L)
    finish(ZD, ZP_L)
    take_d(D_R, (1,), (D_WR, up))
    products(y, ER, [(ER, sp(D_R), False)], tiles=[(full, top)])
    take(Z_UR)
    products(y, ER, [(sp(M_UR), sp(Z_UR), False)])
    finish(ER, quads=(0, 2))
    take_d(D_R, (3,), (D_WR, up))
    products(y, ER, [(ER, sp(D_R), False)], tiles=[(full, low)])
    finish(ER, quads=(1, 3))
    finish(ML, Q_L, (0, 1))
    take_d(D_WR, (0, 1))
    products(y, PR, [(PR, sp(D_WR), False)], tiles=[(full, top)])
    finish(PR, quads=(0, 2))
    finish(ML, Q_L, (2,))
    take_d(D_WR, (3,))
    products(y, PR, [(PR, sp(D_WR), False)], tiles=[(full, low)])
    finish(PR, quads=(1, 3))
    finish(ML, Q_L, (3,))

    for copy in small:
        copy.wait_send()
    for copy in sent.values():
        copy.wait_send()


def write(y, out, zero, sem):
    zero[...] = jnp.zeros_like(zero)
    copies = [(z, slot) for z in range(2) for slot in range(14)]
    started = []
    for t in range(5):
        for q in DQUADS if t == DG else range(4):
            z, z2 = QUADS[q]
            slot = (1 if q == 1 else 0) if t == DG else block_slot(t, z, z2)
            copies.remove((z, slot))
            started.append((y.at[t, pl.ds(z * B, B), pl.ds(z2 * B, B)], z, slot))
    started = [
        pltpu.make_async_copy(source, out.at[z, slot], sem.at[z * 14 + slot])
        for source, z, slot in started + [(zero, z, slot) for z, slot in copies]
    ]
    for copy in started:
        copy.start()
    for copy in started:
        copy.wait()


def shards(stored_blocks, onsite, bond_mask):
    squared = pl.pallas_call(
        kernel,
        out_shape=pltpu.VMEM((5, W2, W2), F32),
        in_specs=[
            pl.BlockSpec(memory_space=pltpu.HBM),
            pl.BlockSpec(memory_space=pltpu.HBM),
            pl.BlockSpec(memory_space=pltpu.HBM),
        ],
        out_specs=pl.BlockSpec(memory_space=pltpu.VMEM),
        scratch_shapes=[
            pltpu.VMEM((5, W2, W2), F32),
            pltpu.VMEM((NRX, W2, W2), F32),
            pltpu.VMEM((NSPLIT, W2, W2), BF16),
            pltpu.VMEM((NSPLIT, W2, W2), BF16),
            pltpu.VMEM((3, W2, W2), F32),
            pltpu.VMEM((3, 2, 128), F32),
            pltpu.VMEM((22, 2, 128), F32),
            pltpu.VMEM((8, B), F32),
            pltpu.VMEM((2, B), F32),
            pltpu.SMEM((2, 13), jnp.int32),
            pltpu.SemaphoreType.DMA((21,)),
            pltpu.SemaphoreType.DMA((NRX * 5,)),
            pltpu.SemaphoreType.DMA((NRX * 5,)),
            pltpu.SemaphoreType.DMA((22,)),
            pltpu.SemaphoreType.DMA((22,)),
            pltpu.SemaphoreType.REGULAR((2,)),
        ],
        compiler_params=pltpu.CompilerParams(
            collective_id=0, has_side_effects=True, vmem_limit_bytes=50 * 1024 * 1024
        ),
        name="sp2_step",
    )(stored_blocks[0, 0], onsite[0, 0], bond_mask[0, 0])
    result = pl.pallas_call(
        write,
        out_shape=jax.ShapeDtypeStruct(stored_blocks.shape[2:], F32),
        in_specs=[pl.BlockSpec(memory_space=pltpu.VMEM)],
        out_specs=pl.BlockSpec(memory_space=pltpu.HBM),
        scratch_shapes=[pltpu.VMEM((B, B), F32), pltpu.SemaphoreType.DMA((28,))],
        compiler_params=pltpu.CompilerParams(vmem_limit_bytes=4 * 1024 * 1024),
        name="write_out",
    )(squared)
    return result[None, None]


def solution(mesh):
    in_specs = (
        P("row", "col", None, None, None, None),
        P("row", "col", None, None),
        P("row", "col", None, None),
    )
    out_specs = P("row", "col", None, None, None, None)
    return jax.shard_map(shards, mesh=mesh, in_specs=in_specs, out_specs=out_specs, check_vma=False)
```

```python
import jax
import jax.numpy as jnp
from jax import lax
from jax.experimental import pallas as pl
from jax.experimental.pallas import tpu as pltpu
from jax.sharding import PartitionSpec as P

MESH = pl.DeviceIdType.MESH
F32 = jnp.float32
BF16 = jnp.bfloat16
B = 256
W2 = 2 * B

DG, ER, ML, ZD, PR = range(5)
MIDDLE = {ER: 3, ML: 6, ZD: 9, PR: 12}
DP, ZP, QQ = range(3)

(DP_L, ZP_L, Q_L, M_R, Z_R, D_R, Z_U, P_U, M_UR, Z_UR, E_W, D_W, D_WR) = range(13)
NRX = 13
ET, P_UT = 5, 6


def sp(rx):
    return 4 + rx


NSPLIT = 4 + NRX

QUADS = ((0, 0), (0, 1), (1, 0), (1, 1))
DQUADS = (0, 1, 3)
SYM = {
    0: ((0, 0, 128, 0, 256), (1, 128, 128, 128, 128)),
    1: ((2, 0, 256, 256, 256),),
    3: ((3, 256, 128, 256, 256), (4, 384, 128, 384, 128)),
}


def block_slot(t, z, z2):
    return MIDDLE[t] + z2 - z


def kernel(stored, onsite_in, mask_in, y, own, rx, hi, lo, handed, part, gath, steer, onsite, mask,
           in_sem, send_sem, recv_sem, ar_send, ar_recv, round_sem):
    row = lax.axis_index("row")
    col = lax.axis_index("col")
    nrow = lax.axis_size("row")
    ncol = lax.axis_size("col")
    right = (row, lax.rem(col + 1, ncol))
    left = (row, lax.rem(col + ncol - 1, ncol))
    down = (lax.rem(row + 1, nrow), col)
    up = (lax.rem(row + nrow - 1, nrow), col)
    col_peers = [(row, lax.rem(col + j, ncol)) for j in range(1, ncol)]
    row_peers = [(lax.rem(row + j, nrow), col) for j in range(1, nrow)]

    near = [(row, lax.rem(col + j, ncol)) for j in (1, ncol - 1, 4, ncol - 4)]
    near += [(lax.rem(row + j, nrow), col) for j in (1, nrow - 1, 2, nrow - 2)]
    barrier = pltpu.get_barrier_semaphore()

    def tell(sem):
        for peer in near:
            pl.semaphore_signal(sem, inc=1, device_id=peer, device_id_type=MESH)

    def heard(sem):
        pl.semaphore_wait(sem, len(near))

    tell(barrier)

    mask_load = pltpu.make_async_copy(mask_in, mask, in_sem.at[19])
    mask_load.start()
    loads = {}
    for t, q in [(t, q) for q in (0, 2, 1, 3) for t in (PR, ML, ER)] + [(ZD, q) for q in range(4)]:
        z, z2 = QUADS[q]
        loads[t, q] = pltpu.make_async_copy(
            stored.at[z, block_slot(t, z, z2)],
            own.at[t, pl.ds(z * B, B), pl.ds(z2 * B, B)],
            in_sem.at[(t - 1) * 4 + q],
        )
    for n, (q, z, slot) in enumerate(((0, 0, 0), (1, 0, 1), (3, 1, 0))):
        i, j = QUADS[q]
        loads[DG, q] = pltpu.make_async_copy(
            stored.at[z, slot], own.at[DG, pl.ds(i * B, B), pl.ds(j * B, B)], in_sem.at[16 + n]
        )
    for copy in loads.values():
        copy.start()

    onsite_load = pltpu.make_async_copy(onsite_in, onsite, in_sem.at[20])
    onsite_load.start()
    mask_load.wait()

    def put_split(k, rows, cols, value):
        high = value.astype(BF16)
        hi[k, rows, cols] = high
        lo[k, rows, cols] = (value - high.astype(F32)).astype(BF16)

    sent = {}

    def send_piece(source, rxi, p, where, peer, start=True):
        copy = pltpu.make_async_remote_copy(
            src_ref=source(*where),
            dst_ref=rx.at[(rxi,) + where],
            send_sem=send_sem.at[rxi * 5 + p],
            recv_sem=recv_sem.at[rxi * 5 + p],
            device_id=peer,
            device_id_type=MESH,
        )
        if start:
            copy.start()
        sent[rxi, p] = copy

    def send(source, rxi, q, peer, start=True):
        i, j = QUADS[q]
        send_piece(source, rxi, q, (pl.ds(i * B, B), pl.ds(j * B, B)), peer, start)

    def send_sym(source, rxi, q, peer, start=True):
        for p, r, nr, c, nc in SYM[q]:
            send_piece(source, rxi, p, (pl.ds(r, nr), pl.ds(c, nc)), peer, start)

    def arrive_sym(rxi, q, forward=None):
        for p, r, nr, c, nc in SYM[q]:
            sent[rxi, p].wait_recv()
            if forward is not None:
                send_piece(from_rx(rxi), forward[0], p, (pl.ds(r, nr), pl.ds(c, nc)), forward[1])
        if q != 1:
            o = 0 if q == 0 else B
            mirrored = rx[rxi, pl.ds(o, 128), pl.ds(o + 128, 128)].T
            rx[rxi, pl.ds(o + 128, 128), pl.ds(o, 128)] = mirrored

    def from_own(t):
        return lambda rows, cols: own.at[t, rows, cols]

    def from_rx(k):
        return lambda rows, cols: rx.at[k, rows, cols]

    def from_handed(k):
        return lambda rows, cols: handed.at[k, rows, cols]

    def own_block(t, q, squares):
        z, z2 = QUADS[q]
        loads[t, q].wait()
        keep = mask[z, block_slot(t, z, z2) - 1].astype(F32)
        cols = pl.ds(z2 * B, B)

        def strip_step(s, total):
            rows = pl.ds(pl.multiple_of(z * B + s * 64, 64), 64)
            value = own[t, rows, cols] * keep
            own[t, rows, cols] = value
            put_split(t, rows, cols, value)
            return total + jnp.sum((value * value).reshape(8, 8, B), axis=0)

        return lax.fori_loop(0, 4, strip_step, squares, unroll=True)

    def prep(rxi, q, flip=None, keep=True):
        i, j = QUADS[q]

        def strip_step(s, carry):
            offset = pl.multiple_of(s * 128, 128)
            value = rx[rxi, pl.ds(i * B + offset, 128), pl.ds(j * B, B)]
            if keep:
                put_split(sp(rxi), pl.ds(i * B + offset, 128), pl.ds(j * B, B), value)
            if flip is not None:
                put_split(flip, pl.ds(j * B, B), pl.ds(i * B + offset, 128), value.T)
            return carry

        lax.fori_loop(0, 2, strip_step, 0)

    def take(rxi, quads=range(4), forward=None, **how):
        for q in quads:
            sent[rxi, q].wait_recv()
            if forward is not None:
                send(from_rx(rxi), forward[0], q, forward[1])
            prep(rxi, q, **how)

    def take_t(rxi, quads=range(4), forward=None):
        take(rxi, quads, forward, flip=sp(rxi), keep=False)

    def take_d(rxi, quads=DQUADS, forward=None):
        for q in quads:
            arrive_sym(rxi, q, forward)
            prep(rxi, q, flip=sp(rxi) if q == 1 else None)

    full = slice(None)

    def products(target, slot, terms, first=False, tiles=None):
        def tile(rows, cols):
            total = None if first else target[slot, rows, cols]
            for a, b, turned in terms:
                a_hi = hi[a, rows, :]
                a_lo = lo[a, rows, :]
                if turned:
                    b_hi, b_lo = hi[b, cols, :], lo[b, cols, :]
                    dims = (((1,), (1,)), ((), ()))
                else:
                    b_hi, b_lo = hi[b, :, cols], lo[b, :, cols]
                    dims = (((1,), (0,)), ((), ()))
                for u, v in ((a_hi, b_hi), (a_hi, b_lo), (a_lo, b_hi)):
                    term = lax.dot_general(u, v, dims, preferred_element_type=F32)
                    total = term if total is None else total + term
            target[slot, rows, cols] = total

        if tiles is not None:
            for rows, cols in tiles:
                tile(rows, cols)
        else:

            def each(n, carry):
                tile(full, pl.ds(pl.multiple_of(n * B, B), B))
                return carry

            lax.fori_loop(0, 2, each, 0)

    def finish(yi, extra=None, quads=range(4)):
        quads = DQUADS if yi == DG else quads
        for q in quads:
            z, z2 = QUADS[q]
            if yi == DG:
                slot = 1 if q == 1 else 0
            else:
                slot = block_slot(yi, z, z2)
            if extra is not None and yi == DG:
                arrive_sym(extra, q)
            elif extra is not None:
                sent[extra, q].wait_recv()
            keep = mask[z, slot - 1].astype(F32) if slot else None

            def strip_step(s, carry, z=z, z2=z2, keep=keep):
                rows = pl.ds(pl.multiple_of(z * B + s * 64, 64), 64)
                cols = pl.ds(z2 * B, B)
                value = y[yi, rows, cols]
                if extra is not None:
                    value = value + rx[extra, rows, cols]
                value = value + steer[0:1, :] * (own[yi, rows, cols] - value)
                if keep is not None:
                    value = value * keep
                y[yi, rows, cols] = value
                return carry

            lax.fori_loop(0, 4, strip_step, 0, unroll=True)

    top, low = pl.ds(0, B), pl.ds(B, B)
    def turn_own(quads):
        for q in quads:
            i, j = QUADS[q]
            value = own[ER, pl.ds(i * B, B), pl.ds(j * B, B)].T
            put_split(ET, pl.ds(j * B, B), pl.ds(i * B, B), value)

    squares = own_block(PR, 0, jnp.zeros((8, B), F32))
    heard(barrier)
    send(from_own(PR), P_U, 0, down)
    tell(round_sem.at[0])
    squares = own_block(ML, 0, squares)
    for q in (0, 1):
        send(from_own(ML), M_R, q, left, start=False)

    def start_m(*quads):
        for q in quads:
            sent[M_R, q].start()

    odd = lax.rem(row, 2) == 1
    even = lax.rem(row, 2) == 0
    pl.when(odd)(lambda: start_m(0))
    squares = own_block(ER, 0, squares)
    send(from_own(ER), E_W, 0, up)
    squares = own_block(PR, 2, squares)
    send(from_own(PR), P_U, 2, down)
    squares = own_block(ER, 2, squares)
    send(from_own(ER), E_W, 2, up)
    squares = own_block(ML, 1, squares)
    pl.when(odd)(lambda: start_m(1))
    turn_own((0, 2))
    squares = own_block(PR, 1, squares)
    send(from_own(PR), P_U, 1, down)
    send_sym(from_handed(DP), DP_L, 0, right, start=False)
    diagonal_sums = [(ET, ET, True), (P_UT, P_UT, True)]

    def start_of_diagonal():
        take(P_U, (0, 2), flip=P_UT)
        products(handed, DP, diagonal_sums, first=True, tiles=[(top, top)])
        for p in (0, 1):
            sent[DP_L, p].start()

    pl.when(odd)(start_of_diagonal)
    squares = own_block(PR, 3, squares)
    send(from_own(PR), P_U, 3, down)
    for q in (1, 3):
        squares = own_block(ER, q, squares)
        send(from_own(ER), E_W, q, up)
    pl.when(even)(lambda: start_m(0, 1))
    heard(round_sem.at[0])
    tell(round_sem.at[1])
    pl.when(even)(start_of_diagonal)
    turn_own((1, 3))
    for q in (1, 3):
        send_sym(from_handed(DP), DP_L, q, right, start=False)

    def rest_of_diagonal():
        take(P_U, (1, 3), flip=P_UT)
        products(handed, DP, diagonal_sums, first=True, tiles=[(full, low)])
        for p in (2, 3, 4):
            sent[DP_L, p].start()

    pl.when(odd)(rest_of_diagonal)
    for q in (2, 3):
        squares = own_block(ML, q, squares)
    send(from_own(ML), M_R, 2, left)
    for q in range(4):
        squares = own_block(ZD, q, squares)
        send(from_own(ZD), Z_U, q, down)
    squares = 2.0 * squares
    trace = jnp.zeros((8, B), F32)
    onsite_load.wait()
    diag = lax.broadcasted_iota(jnp.int32, (B, B), 0) == lax.broadcasted_iota(jnp.int32, (B, B), 1)
    for z, q in ((0, 0), (1, 3)):
        loads[DG, q].wait()
        here = pl.ds(z * B, B)
        raw = own[DG, here, here]
        value = 0.5 * (raw + raw.T) + jnp.where(diag, onsite[z : z + 1, :], 0.0)
        own[DG, here, here] = value
        put_split(DG, here, here, value)
        squares = squares + jnp.sum((value * value).reshape(32, 8, B), axis=0)
        trace = trace + jnp.sum(jnp.where(diag, value, 0.0).reshape(32, 8, B), axis=0)
    loads[DG, 1].wait()
    value = own[DG, top, low] * mask[0, 0].astype(F32)
    own[DG, top, low] = value
    put_split(DG, top, low, value)
    squares = squares + 2.0 * jnp.sum((value * value).reshape(32, 8, B), axis=0)
    flipped = value.T
    own[DG, low, top] = flipped
    put_split(DG, low, top, flipped)
    trace = trace[:, :128] + trace[:, 128:]
    squares = squares[:, :128] + squares[:, 128:]
    part[0, 0:1, :] = jnp.sum(trace, axis=0, keepdims=True)
    part[0, 1:2, :] = jnp.sum(squares, axis=0, keepdims=True)

    small = []

    def send_part(stage, peers, base):
        copies = []
        for n, peer in enumerate(peers):
            copy = pltpu.make_async_remote_copy(
                src_ref=part.at[stage],
                dst_ref=gath.at[base + n],
                send_sem=ar_send.at[base + n],
                recv_sem=ar_recv.at[base + n],
                device_id=peer,
                device_id_type=MESH,
            )
            copy.start()
            copies.append(copy)
        small.extend(copies)
        return copies

    def add_parts(stage, copies, base):
        total = part[stage]
        for n, copy in enumerate(copies):
            copy.wait_recv()
            total = total + gath[base + n]
        part[stage + 1] = total

    heard(round_sem.at[1])
    col_parts = send_part(0, col_peers, 0)
    send(from_own(ML), M_R, 3, left)
    for q in range(4):
        send(from_own(ZD), Z_R, q, left)
    for q in DQUADS:
        send_sym(from_own(DG), D_W, q, up)
        send_sym(from_own(DG), D_R, q, left)

    products(handed, ZP, [(ET, PR, False)], first=True)
    pl.when(even)(rest_of_diagonal)

    take(M_R, (0, 1), (M_UR, down))
    for q, quads, cols in ((0, (0, 2), top), (1, (1, 3), low)):
        take(E_W, quads)
        products(handed, ZP, [(sp(M_R), sp(E_W), False)], tiles=[(top, cols)])
        send(from_handed(ZP), ZP_L, q, right)
    products(y, ER, [(DG, ER, False)], first=True)
    products(y, ML, [(DG, ML, False)], first=True)
    take(M_R, (2, 3), (M_UR, down))
    for q, cols in ((2, top), (3, low)):
        products(handed, ZP, [(sp(M_R), sp(E_W), False)], tiles=[(low, cols)])
        send(from_handed(ZP), ZP_L, q, right)
    products(
        y,
        DG,
        [(DG, DG, False), (ER, ER, True), (ML, ML, True), (ZD, ZD, True), (PR, PR, True)],
        first=True,
        tiles=[(top, top), (full, low)],
    )
    add_parts(0, col_parts, 0)
    row_parts = send_part(1, row_peers, 15)
    take_d(D_W)
    products(handed, QQ, [(ET, ZD, False), (sp(M_R), sp(D_W), False)], first=True)
    products(y, PR, [(DG, PR, False), (ZD, sp(E_W), False)], first=True)
    take(Z_R, (0, 1), (Z_UR, down))
    for q, cols in ((0, top), (1, low)):
        products(handed, QQ, [(sp(Z_R), sp(E_W), True)], tiles=[(top, cols)])
        send(from_handed(QQ), Q_L, q, right)
    products(
        y,
        ZD,
        [(DG, ZD, False), (ZD, sp(D_W), False), (ER, sp(M_R), False), (PR, sp(E_W), True)],
        first=True,
    )
    take(Z_R, (2,), (Z_UR, down))
    take_t(Z_U)
    products(y, ER, [(ZD, sp(M_R), True), (sp(Z_U), sp(P_U), False)])
    take(Z_R, (3,), (Z_UR, down))
    for q, cols in ((2, top), (3, low)):
        products(handed, QQ, [(sp(Z_R), sp(E_W), True)], tiles=[(low, cols)])
        send(from_handed(QQ), Q_L, q, right)
    take_t(M_UR)
    products(
        y,
        DG,
        [(sp(Z_U), sp(Z_U), True), (sp(M_UR), sp(M_UR), True)],
        tiles=[(top, top), (full, low)],
    )
    add_parts(1, row_parts, 15)
    total = part[2]
    t1 = jnp.sum(total[0:1, :])
    t2 = jnp.sum(total[1:2, :])
    goal = float(nrow * ncol * B)
    lean = (jnp.abs(t2 - goal) - jnp.abs(2.0 * t1 - t2 - goal)) / B
    steer[...] = 2.0 / (1.0 + jnp.exp(-jnp.full((8, B), lean, F32)))
    take_d(D_R, (0,), (D_WR, up))
    products(y, ER, [(PR, sp(Z_R), True)])
    products(y, PR, [(ER, sp(Z_R), False)])
    finish(DG, DP_L)
    finish(ZD, ZP_L)
    take_d(D_R, (1,), (D_WR, up))
    products(y, ER, [(ER, sp(D_R), False)], tiles=[(full, top)])
    take(Z_UR)
    products(y, ER, [(sp(M_UR), sp(Z_UR), False)])
    finish(ER, quads=(0, 2))
    take_d(D_R, (3,), (D_WR, up))
    products(y, ER, [(ER, sp(D_R), False)], tiles=[(full, low)])
    finish(ER, quads=(1, 3))
    finish(ML, Q_L, (0, 1))
    take_d(D_WR, (0, 1))
    products(y, PR, [(PR, sp(D_WR), False)], tiles=[(full, top)])
    finish(PR, quads=(0, 2))
    finish(ML, Q_L, (2,))
    take_d(D_WR, (3,))
    products(y, PR, [(PR, sp(D_WR), False)], tiles=[(full, low)])
    finish(PR, quads=(1, 3))
    finish(ML, Q_L, (3,))

    for copy in small:
        copy.wait_send()
    for copy in sent.values():
        copy.wait_send()


def write(y, out, zero, sem):
    zero[...] = jnp.zeros_like(zero)
    copies = [(z, slot) for z in range(2) for slot in range(14)]
    started = []
    for t in range(5):
        for q in DQUADS if t == DG else range(4):
            z, z2 = QUADS[q]
            slot = (1 if q == 1 else 0) if t == DG else block_slot(t, z, z2)
            copies.remove((z, slot))
            started.append((y.at[t, pl.ds(z * B, B), pl.ds(z2 * B, B)], z, slot))
    started = [
        pltpu.make_async_copy(source, out.at[z, slot], sem.at[z * 14 + slot])
        for source, z, slot in started + [(zero, z, slot) for z, slot in copies]
    ]
    for copy in started:
        copy.start()
    for copy in started:
        copy.wait()


def shards(stored_blocks, onsite, bond_mask):
    squared = pl.pallas_call(
        kernel,
        out_shape=pltpu.VMEM((5, W2, W2), F32),
        in_specs=[
            pl.BlockSpec(memory_space=pltpu.HBM),
            pl.BlockSpec(memory_space=pltpu.HBM),
            pl.BlockSpec(memory_space=pltpu.HBM),
        ],
        out_specs=pl.BlockSpec(memory_space=pltpu.VMEM),
        scratch_shapes=[
            pltpu.VMEM((5, W2, W2), F32),
            pltpu.VMEM((NRX, W2, W2), F32),
            pltpu.VMEM((NSPLIT, W2, W2), BF16),
            pltpu.VMEM((NSPLIT, W2, W2), BF16),
            pltpu.VMEM((3, W2, W2), F32),
            pltpu.VMEM((3, 2, 128), F32),
            pltpu.VMEM((22, 2, 128), F32),
            pltpu.VMEM((8, B), F32),
            pltpu.VMEM((2, B), F32),
            pltpu.SMEM((2, 13), jnp.int32),
            pltpu.SemaphoreType.DMA((21,)),
            pltpu.SemaphoreType.DMA((NRX * 5,)),
            pltpu.SemaphoreType.DMA((NRX * 5,)),
            pltpu.SemaphoreType.DMA((22,)),
            pltpu.SemaphoreType.DMA((22,)),
            pltpu.SemaphoreType.REGULAR((2,)),
        ],
        compiler_params=pltpu.CompilerParams(
            collective_id=0, has_side_effects=True, vmem_limit_bytes=50 * 1024 * 1024
        ),
        name="sp2_step",
    )(stored_blocks[0, 0], onsite[0, 0], bond_mask[0, 0])
    result = pl.pallas_call(
        write,
        out_shape=jax.ShapeDtypeStruct(stored_blocks.shape[2:], F32),
        in_specs=[pl.BlockSpec(memory_space=pltpu.VMEM)],
        out_specs=pl.BlockSpec(memory_space=pltpu.HBM),
        scratch_shapes=[pltpu.VMEM((B, B), F32), pltpu.SemaphoreType.DMA((28,))],
        compiler_params=pltpu.CompilerParams(vmem_limit_bytes=4 * 1024 * 1024),
        name="write_out",
    )(squared)
    return result[None, None]


def solution(mesh):
    in_specs = (
        P("row", "col", None, None, None, None),
        P("row", "col", None, None),
        P("row", "col", None, None),
    )
    out_specs = P("row", "col", None, None, None, None)
    return jax.shard_map(shards, mesh=mesh, in_specs=in_specs, out_specs=out_specs, check_vma=False)
```

```python
import jax
import jax.numpy as jnp
from jax import lax
from jax.experimental import pallas as pl
from jax.experimental.pallas import tpu as pltpu
from jax.sharding import PartitionSpec as P

MESH = pl.DeviceIdType.MESH
F32 = jnp.float32
BF16 = jnp.bfloat16
B = 256
W2 = 2 * B

DG, ER, ML, ZD, PR = range(5)
MIDDLE = {ER: 3, ML: 6, ZD: 9, PR: 12}
DP, ZP, QQ = range(3)

(DP_L, ZP_L, Q_L, M_R, Z_R, D_R, Z_U, P_U, M_UR, Z_UR, E_W, D_W, D_WR) = range(13)
NRX = 13
ET, P_UT = 5, 6


def sp(rx):
    return 4 + rx


NSPLIT = 4 + NRX

QUADS = ((0, 0), (0, 1), (1, 0), (1, 1))
DQUADS = (0, 1, 3)
SYM = {
    0: ((0, 0, 128, 0, 256), (1, 128, 128, 128, 128)),
    1: ((2, 0, 256, 256, 256),),
    3: ((3, 256, 128, 256, 256), (4, 384, 128, 384, 128)),
}


def block_slot(t, z, z2):
    return MIDDLE[t] + z2 - z


def kernel(stored, onsite_in, mask_in, y, own, rx, hi, lo, handed, part, gath, steer, onsite, mask,
           in_sem, send_sem, recv_sem, ar_send, ar_recv, round_sem):
    row = lax.axis_index("row")
    col = lax.axis_index("col")
    nrow = lax.axis_size("row")
    ncol = lax.axis_size("col")
    right = (row, lax.rem(col + 1, ncol))
    left = (row, lax.rem(col + ncol - 1, ncol))
    down = (lax.rem(row + 1, nrow), col)
    up = (lax.rem(row + nrow - 1, nrow), col)
    col_peers = [(row, lax.rem(col + j, ncol)) for j in range(1, ncol)]
    row_peers = [(lax.rem(row + j, nrow), col) for j in range(1, nrow)]

    near = [(row, lax.rem(col + j, ncol)) for j in (1, ncol - 1, 4, ncol - 4)]
    near += [(lax.rem(row + j, nrow), col) for j in (1, nrow - 1, 2, nrow - 2)]
    barrier = pltpu.get_barrier_semaphore()

    def tell(sem):
        for peer in near:
            pl.semaphore_signal(sem, inc=1, device_id=peer, device_id_type=MESH)

    def heard(sem):
        pl.semaphore_wait(sem, len(near))

    tell(barrier)

    mask_load = pltpu.make_async_copy(mask_in, mask, in_sem.at[19])
    mask_load.start()
    loads = {}
    for t, q in [(t, q) for q in (0, 2, 1, 3) for t in (PR, ML, ER)] + [(ZD, q) for q in range(4)]:
        z, z2 = QUADS[q]
        loads[t, q] = pltpu.make_async_copy(
            stored.at[z, block_slot(t, z, z2)],
            own.at[t, pl.ds(z * B, B), pl.ds(z2 * B, B)],
            in_sem.at[(t - 1) * 4 + q],
        )
    for n, (q, z, slot) in enumerate(((0, 0, 0), (1, 0, 1), (3, 1, 0))):
        i, j = QUADS[q]
        loads[DG, q] = pltpu.make_async_copy(
            stored.at[z, slot], own.at[DG, pl.ds(i * B, B), pl.ds(j * B, B)], in_sem.at[16 + n]
        )
    for copy in loads.values():
        copy.start()

    onsite_load = pltpu.make_async_copy(onsite_in, onsite, in_sem.at[20])
    onsite_load.start()
    mask_load.wait()

    def put_split(k, rows, cols, value):
        high = value.astype(BF16)
        hi[k, rows, cols] = high
        lo[k, rows, cols] = (value - high.astype(F32)).astype(BF16)

    sent = {}

    def send_piece(source, rxi, p, where, peer, start=True):
        copy = pltpu.make_async_remote_copy(
            src_ref=source(*where),
            dst_ref=rx.at[(rxi,) + where],
            send_sem=send_sem.at[rxi * 5 + p],
            recv_sem=recv_sem.at[rxi * 5 + p],
            device_id=peer,
            device_id_type=MESH,
        )
        if start:
            copy.start()
        sent[rxi, p] = copy

    def send(source, rxi, q, peer, start=True):
        i, j = QUADS[q]
        send_piece(source, rxi, q, (pl.ds(i * B, B), pl.ds(j * B, B)), peer, start)

    def send_sym(source, rxi, q, peer, start=True):
        for p, r, nr, c, nc in SYM[q]:
            send_piece(source, rxi, p, (pl.ds(r, nr), pl.ds(c, nc)), peer, start)

    def arrive_sym(rxi, q, forward=None):
        for p, r, nr, c, nc in SYM[q]:
            sent[rxi, p].wait_recv()
            if forward is not None:
                send_piece(from_rx(rxi), forward[0], p, (pl.ds(r, nr), pl.ds(c, nc)), forward[1])
        if q != 1:
            o = 0 if q == 0 else B
            mirrored = rx[rxi, pl.ds(o, 128), pl.ds(o + 128, 128)].T
            rx[rxi, pl.ds(o + 128, 128), pl.ds(o, 128)] = mirrored

    def from_own(t):
        return lambda rows, cols: own.at[t, rows, cols]

    def from_rx(k):
        return lambda rows, cols: rx.at[k, rows, cols]

    def from_handed(k):
        return lambda rows, cols: handed.at[k, rows, cols]

    def own_block(t, q, squares):
        z, z2 = QUADS[q]
        loads[t, q].wait()
        keep = mask[z, block_slot(t, z, z2) - 1].astype(F32)
        cols = pl.ds(z2 * B, B)

        def strip_step(s, total):
            rows = pl.ds(pl.multiple_of(z * B + s * 64, 64), 64)
            value = own[t, rows, cols] * keep
            own[t, rows, cols] = value
            put_split(t, rows, cols, value)
            return total + jnp.sum((value * value).reshape(8, 8, B), axis=0)

        return lax.fori_loop(0, 4, strip_step, squares, unroll=True)

    def prep(rxi, q, flip=None, keep=True):
        i, j = QUADS[q]

        def strip_step(s, carry):
            offset = pl.multiple_of(s * 128, 128)
            value = rx[rxi, pl.ds(i * B + offset, 128), pl.ds(j * B, B)]
            if keep:
                put_split(sp(rxi), pl.ds(i * B + offset, 128), pl.ds(j * B, B), value)
            if flip is not None:
                put_split(flip, pl.ds(j * B, B), pl.ds(i * B + offset, 128), value.T)
            return carry

        lax.fori_loop(0, 2, strip_step, 0)

    def take(rxi, quads=range(4), forward=None, **how):
        for q in quads:
            sent[rxi, q].wait_recv()
            if forward is not None:
                send(from_rx(rxi), forward[0], q, forward[1])
            prep(rxi, q, **how)

    def take_t(rxi, quads=range(4), forward=None):
        take(rxi, quads, forward, flip=sp(rxi), keep=False)

    def take_d(rxi, quads=DQUADS, forward=None):
        for q in quads:
            arrive_sym(rxi, q, forward)
            prep(rxi, q, flip=sp(rxi) if q == 1 else None)

    full = slice(None)

    def products(target, slot, terms, first=False, tiles=None):
        def tile(rows, cols):
            total = None if first else target[slot, rows, cols]
            for a, b, turned in terms:
                a_hi = hi[a, rows, :]
                a_lo = lo[a, rows, :]
                if turned:
                    b_hi, b_lo = hi[b, cols, :], lo[b, cols, :]
                    dims = (((1,), (1,)), ((), ()))
                else:
                    b_hi, b_lo = hi[b, :, cols], lo[b, :, cols]
                    dims = (((1,), (0,)), ((), ()))
                for u, v in ((a_hi, b_hi), (a_hi, b_lo), (a_lo, b_hi)):
                    term = lax.dot_general(u, v, dims, preferred_element_type=F32)
                    total = term if total is None else total + term
            target[slot, rows, cols] = total

        if tiles is not None:
            for rows, cols in tiles:
                tile(rows, cols)
        else:

            def each(n, carry):
                tile(full, pl.ds(pl.multiple_of(n * B, B), B))
                return carry

            lax.fori_loop(0, 2, each, 0)

    def finish(yi, extra=None, quads=range(4)):
        quads = DQUADS if yi == DG else quads
        for q in quads:
            z, z2 = QUADS[q]
            if yi == DG:
                slot = 1 if q == 1 else 0
            else:
                slot = block_slot(yi, z, z2)
            if extra is not None and yi == DG:
                arrive_sym(extra, q)
            elif extra is not None:
                sent[extra, q].wait_recv()
            keep = mask[z, slot - 1].astype(F32) if slot else None

            def strip_step(s, carry, z=z, z2=z2, keep=keep):
                rows = pl.ds(pl.multiple_of(z * B + s * 64, 64), 64)
                cols = pl.ds(z2 * B, B)
                value = y[yi, rows, cols]
                if extra is not None:
                    value = value + rx[extra, rows, cols]
                value = value + steer[0:1, :] * (own[yi, rows, cols] - value)
                if keep is not None:
                    value = value * keep
                y[yi, rows, cols] = value
                return carry

            lax.fori_loop(0, 4, strip_step, 0, unroll=True)

    top, low = pl.ds(0, B), pl.ds(B, B)
    def turn_own(quads):
        for q in quads:
            i, j = QUADS[q]
            value = own[ER, pl.ds(i * B, B), pl.ds(j * B, B)].T
            put_split(ET, pl.ds(j * B, B), pl.ds(i * B, B), value)

    squares = own_block(PR, 0, jnp.zeros((8, B), F32))
    heard(barrier)
    send(from_own(PR), P_U, 0, down)
    tell(round_sem.at[0])
    squares = own_block(ML, 0, squares)
    for q in (0, 1):
        send(from_own(ML), M_R, q, left, start=False)

    def start_m(*quads):
        for q in quads:
            sent[M_R, q].start()

    odd = lax.rem(row, 2) == 1
    even = lax.rem(row, 2) == 0
    pl.when(odd)(lambda: start_m(0))
    squares = own_block(ER, 0, squares)
    send(from_own(ER), E_W, 0, up)
    squares = own_block(PR, 2, squares)
    send(from_own(PR), P_U, 2, down)
    squares = own_block(ER, 2, squares)
    send(from_own(ER), E_W, 2, up)
    squares = own_block(ML, 1, squares)
    pl.when(odd)(lambda: start_m(1))
    turn_own((0, 2))
    squares = own_block(PR, 1, squares)
    send(from_own(PR), P_U, 1, down)
    send_sym(from_handed(DP), DP_L, 0, right, start=False)
    diagonal_sums = [(ET, ET, True), (P_UT, P_UT, True)]

    def start_of_diagonal():
        take(P_U, (0, 2), flip=P_UT)
        products(handed, DP, diagonal_sums, first=True, tiles=[(top, top)])
        for p in (0, 1):
            sent[DP_L, p].start()

    pl.when(odd)(start_of_diagonal)
    squares = own_block(PR, 3, squares)
    send(from_own(PR), P_U, 3, down)
    for q in (1, 3):
        squares = own_block(ER, q, squares)
        send(from_own(ER), E_W, q, up)
    pl.when(even)(lambda: start_m(0, 1))
    heard(round_sem.at[0])
    tell(round_sem.at[1])
    pl.when(even)(start_of_diagonal)
    turn_own((1, 3))
    for q in (1, 3):
        send_sym(from_handed(DP), DP_L, q, right, start=False)

    def rest_of_diagonal():
        take(P_U, (1, 3), flip=P_UT)
        products(handed, DP, diagonal_sums, first=True, tiles=[(full, low)])
        for p in (2, 3, 4):
            sent[DP_L, p].start()

    def own_zp():
        products(handed, ZP, [(ET, PR, False)], first=True)

    for q in (0, 1):
        send(from_rx(M_R), M_UR, q, down, start=False)
        send(from_handed(ZP), ZP_L, q, right, start=False)

    def top_of_zp():
        for q in (0, 1):
            sent[M_R, q].wait_recv()
            sent[M_UR, q].start()
            prep(M_R, q)
        for q, quads, cols in ((0, (0, 2), top), (1, (1, 3), low)):
            take(E_W, quads)
            products(handed, ZP, [(sp(M_R), sp(E_W), False)], tiles=[(top, cols)])
            sent[ZP_L, q].start()

    pl.when(odd)(rest_of_diagonal)
    squares = own_block(ML, 2, squares)
    send(from_own(ML), M_R, 2, left)
    pl.when(odd)(own_zp)
    pl.when(odd)(top_of_zp)
    squares = own_block(ML, 3, squares)
    for q in range(4):
        squares = own_block(ZD, q, squares)
        send(from_own(ZD), Z_U, q, down)
    squares = 2.0 * squares
    trace = jnp.zeros((8, B), F32)
    onsite_load.wait()
    diag = lax.broadcasted_iota(jnp.int32, (B, B), 0) == lax.broadcasted_iota(jnp.int32, (B, B), 1)
    for z, q in ((0, 0), (1, 3)):
        loads[DG, q].wait()
        here = pl.ds(z * B, B)
        raw = own[DG, here, here]
        value = 0.5 * (raw + raw.T) + jnp.where(diag, onsite[z : z + 1, :], 0.0)
        own[DG, here, here] = value
        put_split(DG, here, here, value)
        squares = squares + jnp.sum((value * value).reshape(32, 8, B), axis=0)
        trace = trace + jnp.sum(jnp.where(diag, value, 0.0).reshape(32, 8, B), axis=0)
    loads[DG, 1].wait()
    value = own[DG, top, low] * mask[0, 0].astype(F32)
    own[DG, top, low] = value
    put_split(DG, top, low, value)
    squares = squares + 2.0 * jnp.sum((value * value).reshape(32, 8, B), axis=0)
    flipped = value.T
    own[DG, low, top] = flipped
    put_split(DG, low, top, flipped)
    trace = trace[:, :128] + trace[:, 128:]
    squares = squares[:, :128] + squares[:, 128:]
    part[0, 0:1, :] = jnp.sum(trace, axis=0, keepdims=True)
    part[0, 1:2, :] = jnp.sum(squares, axis=0, keepdims=True)

    small = []

    def send_part(stage, peers, base):
        copies = []
        for n, peer in enumerate(peers):
            copy = pltpu.make_async_remote_copy(
                src_ref=part.at[stage],
                dst_ref=gath.at[base + n],
                send_sem=ar_send.at[base + n],
                recv_sem=ar_recv.at[base + n],
                device_id=peer,
                device_id_type=MESH,
            )
            copy.start()
            copies.append(copy)
        small.extend(copies)
        return copies

    def add_parts(stage, copies, base):
        total = part[stage]
        for n, copy in enumerate(copies):
            copy.wait_recv()
            total = total + gath[base + n]
        part[stage + 1] = total

    heard(round_sem.at[1])
    col_parts = send_part(0, col_peers, 0)
    send(from_own(ML), M_R, 3, left)
    for q in range(4):
        send(from_own(ZD), Z_R, q, left)
    for q in DQUADS:
        send_sym(from_own(DG), D_W, q, up)
        send_sym(from_own(DG), D_R, q, left)

    pl.when(even)(own_zp)
    pl.when(even)(rest_of_diagonal)
    pl.when(even)(top_of_zp)
    products(y, ER, [(DG, ER, False)], first=True)
    products(y, ML, [(DG, ML, False)], first=True)
    take(M_R, (2, 3), (M_UR, down))
    for q, cols in ((2, top), (3, low)):
        products(handed, ZP, [(sp(M_R), sp(E_W), False)], tiles=[(low, cols)])
        send(from_handed(ZP), ZP_L, q, right)
    products(
        y,
        DG,
        [(DG, DG, False), (ER, ER, True), (ML, ML, True), (ZD, ZD, True), (PR, PR, True)],
        first=True,
        tiles=[(top, top), (full, low)],
    )
    add_parts(0, col_parts, 0)
    row_parts = send_part(1, row_peers, 15)
    take_d(D_W)
    products(handed, QQ, [(ET, ZD, False), (sp(M_R), sp(D_W), False)], first=True)
    products(y, PR, [(DG, PR, False), (ZD, sp(E_W), False)], first=True)
    take(Z_R, (0, 1), (Z_UR, down))
    for q, cols in ((0, top), (1, low)):
        products(handed, QQ, [(sp(Z_R), sp(E_W), True)], tiles=[(top, cols)])
        send(from_handed(QQ), Q_L, q, right)
    products(
        y,
        ZD,
        [(DG, ZD, False), (ZD, sp(D_W), False), (ER, sp(M_R), False), (PR, sp(E_W), True)],
        first=True,
    )
    take(Z_R, (2,), (Z_UR, down))
    take_t(Z_U)
    products(y, ER, [(ZD, sp(M_R), True), (sp(Z_U), sp(P_U), False)])
    take(Z_R, (3,), (Z_UR, down))
    for q, cols in ((2, top), (3, low)):
        products(handed, QQ, [(sp(Z_R), sp(E_W), True)], tiles=[(low, cols)])
        send(from_handed(QQ), Q_L, q, right)
    take_t(M_UR)
    products(
        y,
        DG,
        [(sp(Z_U), sp(Z_U), True), (sp(M_UR), sp(M_UR), True)],
        tiles=[(top, top), (full, low)],
    )
    add_parts(1, row_parts, 15)
    total = part[2]
    t1 = jnp.sum(total[0:1, :])
    t2 = jnp.sum(total[1:2, :])
    goal = float(nrow * ncol * B)
    lean = (jnp.abs(t2 - goal) - jnp.abs(2.0 * t1 - t2 - goal)) / B
    steer[...] = 2.0 / (1.0 + jnp.exp(-jnp.full((8, B), lean, F32)))
    take_d(D_R, (0,), (D_WR, up))
    products(y, ER, [(PR, sp(Z_R), True)])
    products(y, PR, [(ER, sp(Z_R), False)])
    finish(DG, DP_L)
    finish(ZD, ZP_L)
    take_d(D_R, (1,), (D_WR, up))
    products(y, ER, [(ER, sp(D_R), False)], tiles=[(full, top)])
    take(Z_UR)
    products(y, ER, [(sp(M_UR), sp(Z_UR), False)])
    finish(ER, quads=(0, 2))
    take_d(D_R, (3,), (D_WR, up))
    products(y, ER, [(ER, sp(D_R), False)], tiles=[(full, low)])
    finish(ER, quads=(1, 3))
    finish(ML, Q_L, (0, 1))
    take_d(D_WR, (0, 1))
    products(y, PR, [(PR, sp(D_WR), False)], tiles=[(full, top)])
    finish(PR, quads=(0, 2))
    finish(ML, Q_L, (2,))
    take_d(D_WR, (3,))
    products(y, PR, [(PR, sp(D_WR), False)], tiles=[(full, low)])
    finish(PR, quads=(1, 3))
    finish(ML, Q_L, (3,))

    for copy in small:
        copy.wait_send()
    for copy in sent.values():
        copy.wait_send()


def write(y, out, zero, sem):
    zero[...] = jnp.zeros_like(zero)
    copies = [(z, slot) for z in range(2) for slot in range(14)]
    started = []
    for t in range(5):
        for q in DQUADS if t == DG else range(4):
            z, z2 = QUADS[q]
            slot = (1 if q == 1 else 0) if t == DG else block_slot(t, z, z2)
            copies.remove((z, slot))
            started.append((y.at[t, pl.ds(z * B, B), pl.ds(z2 * B, B)], z, slot))
    started = [
        pltpu.make_async_copy(source, out.at[z, slot], sem.at[z * 14 + slot])
        for source, z, slot in started + [(zero, z, slot) for z, slot in copies]
    ]
    for copy in started:
        copy.start()
    for copy in started:
        copy.wait()


def shards(stored_blocks, onsite, bond_mask):
    squared = pl.pallas_call(
        kernel,
        out_shape=pltpu.VMEM((5, W2, W2), F32),
        in_specs=[
            pl.BlockSpec(memory_space=pltpu.HBM),
            pl.BlockSpec(memory_space=pltpu.HBM),
            pl.BlockSpec(memory_space=pltpu.HBM),
        ],
        out_specs=pl.BlockSpec(memory_space=pltpu.VMEM),
        scratch_shapes=[
            pltpu.VMEM((5, W2, W2), F32),
            pltpu.VMEM((NRX, W2, W2), F32),
            pltpu.VMEM((NSPLIT, W2, W2), BF16),
            pltpu.VMEM((NSPLIT, W2, W2), BF16),
            pltpu.VMEM((3, W2, W2), F32),
            pltpu.VMEM((3, 2, 128), F32),
            pltpu.VMEM((22, 2, 128), F32),
            pltpu.VMEM((8, B), F32),
            pltpu.VMEM((2, B), F32),
            pltpu.SMEM((2, 13), jnp.int32),
            pltpu.SemaphoreType.DMA((21,)),
            pltpu.SemaphoreType.DMA((NRX * 5,)),
            pltpu.SemaphoreType.DMA((NRX * 5,)),
            pltpu.SemaphoreType.DMA((22,)),
            pltpu.SemaphoreType.DMA((22,)),
            pltpu.SemaphoreType.REGULAR((2,)),
        ],
        compiler_params=pltpu.CompilerParams(
            collective_id=0, has_side_effects=True, vmem_limit_bytes=50 * 1024 * 1024
        ),
        name="sp2_step",
    )(stored_blocks[0, 0], onsite[0, 0], bond_mask[0, 0])
    result = pl.pallas_call(
        write,
        out_shape=jax.ShapeDtypeStruct(stored_blocks.shape[2:], F32),
        in_specs=[pl.BlockSpec(memory_space=pltpu.VMEM)],
        out_specs=pl.BlockSpec(memory_space=pltpu.HBM),
        scratch_shapes=[pltpu.VMEM((B, B), F32), pltpu.SemaphoreType.DMA((28,))],
        compiler_params=pltpu.CompilerParams(vmem_limit_bytes=4 * 1024 * 1024),
        name="write_out",
    )(squared)
    return result[None, None]


def solution(mesh):
    in_specs = (
        P("row", "col", None, None, None, None),
        P("row", "col", None, None),
        P("row", "col", None, None),
    )
    out_specs = P("row", "col", None, None, None, None)
    return jax.shard_map(shards, mesh=mesh, in_specs=in_specs, out_specs=out_specs, check_vma=False)
```
